128 devices in a mesh: layer: 4 (over x), head: 32 (over y, z, core).
Axes of the slice: x: 4, y: 4, z: 4, core: 2. Of those that a mesh axis runs over, the one named last changes fastest.
Arguments:
- momentum: bfloat16 [4, 32768, 512], P(None, ('layer', 'head')), may hold values from -6 to 6
- grad_one: bfloat16 [4, 32768, 512], P(None, ('layer', 'head')), may hold values from -6 to 6
- grad_two: bfloat16 [4, 32768, 512], P(None, ('layer', 'head')), may hold values from -60 to 60
Outputs:
- update_one: float32 [4, 32768, 512], P(None, ('layer', 'head'))
- update_two: float32 [4, 32768, 512], P(None, ('layer', 'head'))
The draws below stay inside these ranges and needn't reach their ends.
All inputs are finite; a program needn't handle non-finite values.
Results may differ from the reference program's by a relative error of at most 0.0065.
Values may be sent and summed in bfloat16 or wider, within the bound.
A program may use at most 64 MiB of HBM per device.

```python
import jax
import jax.numpy as jnp
from jax import lax

LATENT = 512
HEADS = 128
HEAD_ROWS = 256
NS_ITERS = 5
ROWS = 32768
LAYERS = 4
N_HEAD = 32
DEVICES = 128


def draw_grad_two(key, part):
    row_index = jnp.arange(ROWS, dtype=jnp.int32)
    block_index = row_index // (ROWS // DEVICES) % N_HEAD
    position = block_index.astype(jnp.float32) / jnp.float32(max(N_HEAD - 1, 1))
    scales = jnp.exp(jnp.log(jnp.float32(8.0)) * position)
    values = jnp.clip(jax.random.normal(key, (LAYERS, ROWS, LATENT), jnp.float32), -6.0, 6.0)
    return (values * scales[None, :, None]).astype(jnp.bfloat16)


def steps_of(rng, extent, pieces, least, largest):
    factor_of = 1.0
    for dim, blocks in pieces:
        heights = jax.random.uniform(jax.random.fold_in(jax.random.fold_in(rng, 6), dim), (blocks,), jnp.float32, least / len(pieces), largest / len(pieces))
        factor_of = factor_of * jnp.repeat(jnp.exp(heights), extent[dim] // blocks).reshape((-1,) + (1,) * (len(extent) - 1 - dim))
    return factor_of


def scatter_about(rng, extent, width, limit, shards=(), kind=jnp.bfloat16):
    array = width * jax.random.normal(rng, extent, jnp.float32)
    if shards:
        array = array * steps_of(rng, extent, shards, -0.22, 0.18)
    return jnp.clip(array, -limit, limit).astype(kind)


def setup_inputs(seed: int = 0) -> dict:
    key_of = jax.random.split(jax.random.key(seed), 4)
    momentum = scatter_about(key_of[0], (LAYERS, ROWS, LATENT), 1.0, 6.0, ((1, 128),))
    grad_one = scatter_about(key_of[1], (LAYERS, ROWS, LATENT), 1.0, 6.0, ((1, 128),))
    grad_two = draw_grad_two(jax.random.fold_in(key_of[3], 71), 0)
    return dict(momentum=momentum, grad_one=grad_one, grad_two=grad_two)


quintic_a = 3.4445
quintic_b = -4.775
quintic_c = 2.0315
norm_epsilon = 1e-07
momentum_decay = 0.95

def block_newton(blocks):
    wide = blocks.astype(jnp.float32)
    squares = lax.optimization_barrier(jnp.sum(jnp.square(wide), axis=(1, 2), keepdims=True))
    current = wide / (jnp.sqrt(squares) + norm_epsilon)
    for iteration in range(NS_ITERS):
        gram_part = jnp.einsum('nrl,nsl->nrs', current, current, precision=lax.Precision.HIGHEST)
        polynomial = quintic_b * gram_part + quintic_c * jnp.einsum('nrs,nst->nrt', gram_part, gram_part, precision=lax.Precision.HIGHEST)
        current = quintic_a * current + jnp.einsum('nrs,nsl->nrl', polynomial, current, precision=lax.Precision.HIGHEST)
    return current

def layer_newton(matrix):
    wide = matrix.astype(jnp.float32)
    squared = jnp.sum(jnp.square(wide))
    current = wide / (jnp.sqrt(squared) + norm_epsilon)
    for iteration in range(NS_ITERS):
        gram_part = jnp.dot(current.T, current, precision=lax.Precision.HIGHEST)
        polynomial = quintic_b * gram_part + quintic_c * jnp.dot(gram_part, gram_part, precision=lax.Precision.HIGHEST)
        current = quintic_a * current + jnp.dot(current, polynomial, precision=lax.Precision.HIGHEST)
    return current

def reference(momentum, grad_one, grad_two):
    momentum_one = (momentum_decay * momentum.astype(jnp.float32) + grad_one.astype(jnp.float32)).astype(jnp.bfloat16)
    momentum_two = (momentum_decay * momentum_one.astype(jnp.float32) + grad_two.astype(jnp.float32)).astype(jnp.bfloat16)
    blocks = momentum_one.reshape(LAYERS * HEADS, HEAD_ROWS, LATENT)
    update_one = block_newton(blocks).reshape(LAYERS, ROWS, LATENT) * jnp.sqrt(jnp.float32(max(HEAD_ROWS, LATENT)))
    layers_out = [layer_newton(momentum_two[index]) for index in range(LAYERS)]
    update_two = jnp.stack(layers_out, axis=0) * jnp.sqrt(jnp.float32(ROWS))
    return (update_one, update_two)
```

```python
import math

import jax
import jax.numpy as jnp
from jax import lax
from jax.sharding import PartitionSpec as P

HEAD_ROWS = 256
NS_ITERS = 5
ROWS = 32768

quintic_a = 3.4445
quintic_b = -4.775
quintic_c = 2.0315
norm_epsilon = 1e-07
momentum_decay = 0.95
PREC = lax.Precision.HIGH


def mm(a, b):
    return jnp.matmul(a, b, precision=PREC, preferred_element_type=jnp.float32)


def polynomial_of(gram):
    eye = jnp.eye(gram.shape[-1], dtype=jnp.float32)
    q = None
    s = gram
    for k in range(NS_ITERS):
        m = quintic_a * eye + quintic_b * s + quintic_c * mm(s, s)
        q = m if q is None else mm(q, m)
        if k < NS_ITERS - 1:
            s = mm(mm(s, m), m)
    return q


def shards(momentum, grad_one, grad_two):
    latent = momentum.shape[-1]
    one = (
        momentum_decay * momentum.astype(jnp.float32) + grad_one.astype(jnp.float32)
    ).astype(jnp.bfloat16)
    two = (
        momentum_decay * one.astype(jnp.float32) + grad_two.astype(jnp.float32)
    ).astype(jnp.bfloat16)
    team = lax.all_to_all(two, "layer", split_axis=0, concat_axis=1, tiled=True)[0]
    g2 = lax.psum(jnp.dot(team.T, team, preferred_element_type=jnp.float32), "head")
    n2 = jnp.sqrt(jnp.trace(g2)) + norm_epsilon
    q2 = polynomial_of(g2 / (n2 * n2)) * (math.sqrt(ROWS) / n2)
    q2 = lax.all_gather(q2, "layer", axis=0)
    g1 = jnp.einsum("nrl,nsl->nrs", one, one, preferred_element_type=jnp.float32)
    n1 = jnp.sqrt(jnp.trace(g1, axis1=1, axis2=2))[:, None, None] + norm_epsilon
    q1 = polynomial_of(g1 / (n1 * n1)) * (math.sqrt(max(HEAD_ROWS, latent)) / n1)
    update_one = mm(q1, one.astype(jnp.float32))
    update_two = mm(two.astype(jnp.float32), q2)
    return (update_one, update_two)


def solution(mesh):
    spec = P(None, ("layer", "head"), None)
    return jax.shard_map(
        shards, mesh=mesh, in_specs=(spec,) * 3, out_specs=(spec,) * 2, check_vma=False
    )
```

```python
import functools
import math

import jax
import jax.numpy as jnp
from jax import lax
from jax.experimental import pallas as pl
from jax.experimental.pallas import tpu as pltpu
from jax.sharding import PartitionSpec as P

NS_ITERS = 5
quintic_a = 3.4445
quintic_b = -4.775
quintic_c = 2.0315
norm_epsilon = 1e-07
momentum_decay = 0.95

bf16 = jnp.bfloat16
f32 = jnp.float32
MESH = pl.DeviceIdType.MESH
LAYERS, ROWS, LATENT = 4, 256, 512
ALL_ROWS = 32768
T = 128
BLOCKS = [(i, j) for i in range(4) for j in range(i, 4)]
HALF = len(BLOCKS) * T // 2
PIECE = HALF // 16
OFFSETS = [(1, 1, 2), (1, 1, 0), (1, 0, 2), (0, 1, 2)]
OFFSETS += [(i, j, z) for z in (1, 3) for i in (0, 1) for j in (0, 1)]
OFFSETS += [(1, 0, 0), (0, 1, 0), (0, 0, 2)]


def split(x):
    high = x.astype(bf16)
    return high, (x - high.astype(f32)).astype(bf16)


def dot(x, y):
    return jnp.dot(x, y, preferred_element_type=f32)


def dot3(x, y):
    return dot(x[0], y[0]) + (dot(x[0], y[1]) + dot(x[1], y[0]))


def mm(x, y):
    return dot3(x, y)


def mm_even(x, y):
    h = x[0].shape[0] // 2
    top = dot3([t[:h] for t in x], y)
    low = dot3([t[h:] for t in x], [t[:, h:] for t in y])
    return jnp.concatenate([top, jnp.concatenate([top[:, h:].T, low], 1)], 0)


def eye(n):
    rows = lax.broadcasted_iota(jnp.int32, (n, n), 0)
    return rows == lax.broadcasted_iota(jnp.int32, (n, n), 1)


def polynomials(grams, product):
    n = grams[0].shape[0]
    diag = jnp.where(eye(n), f32(quintic_a), f32(0.0))
    s, q = list(grams), [None] * len(grams)
    for k in range(NS_ITERS):
        parts = [split(t) for t in s]
        m = [
            diag + (quintic_b * t + quintic_c * product(u, u)) for t, u in zip(s, parts)
        ]
        ms = [split(t) for t in m]
        if k < NS_ITERS - 1:
            r = [split(product(u, v)) for u, v in zip(parts, ms)]
            s = [product(u, v) for u, v in zip(r, ms)]
        q = m if k == 0 else [product(split(u), v) for u, v in zip(q, ms)]
    return q


def trace(x):
    return jnp.sum(jnp.where(eye(x.shape[0]), x, f32(0.0)))


def exchange(
    m_ref, g1_ref, g2_ref, y1_ref, y2_ref, q1_ref, q2_ref,
    rx, part, core_in, own, rs, gath, packed, rxq,
    s_row, r_row, s_core, r_core, s_rs, r_rs, s_ag, r_ag, s_rel, r_rel, s_q, r_q,
):
    x = lax.axis_index("layer")
    head = lax.axis_index("head")
    y, z, c = head // 8, (head // 2) % 4, head % 2
    b0, b1 = (x + z) % 2, (y + z) % 2
    lay = b0 + 2 * b1
    lays = [(1 - b0) + 2 * b1, b0 + 2 * (1 - b1), (1 - b0) + 2 * (1 - b1)]
    i, j = x // 2, y // 2
    t = (i * 2 + j) * 4 + z

    def at(x, y, z, c):
        return (x, (y * 4 + z) * 2 + c)

    steps = []
    for a in range(3):
        for s in range(2):
            d = 1 if s == 0 else 3
            steps.append(((x + d) % 4 if a == 0 else x, (y + d) % 4 if a == 1 else y,
                          (z + d) % 4 if a == 2 else z))
    team = []
    for di, dj, dz in OFFSETS:
        i2, j2, z2 = (i + di) % 2, (j + dj) % 2, (z + dz) % 4
        team.append(((2 * i2 + (b0 + z2) % 2, 2 * j2 + (b1 + z2) % 2, z2),
                     (i2 * 2 + j2) * 4 + z2))
    partner = at(x, y, z, 1 - c)

    barrier = pltpu.get_barrier_semaphore()
    greet = [partner]
    greet += [at(*p, k) for p in steps for k in (c, 1 - c)]
    greet += [at(*p, c) for p, _ in team]
    for who in greet:
        pl.semaphore_signal(barrier, inc=1, device_id=who, device_id_type=MESH)

    for n in range(LAYERS):
        one = (momentum_decay * m_ref[n].astype(f32) + g1_ref[n].astype(f32)).astype(bf16)
        y1_ref[n] = one
        y2_ref[n] = (momentum_decay * one.astype(f32) + g2_ref[n].astype(f32)).astype(bf16)

    pl.semaphore_wait(barrier, len(greet))

    def send(src, dst, ss, rr, who):
        return pltpu.make_async_remote_copy(
            src_ref=src, dst_ref=dst, send_sem=ss, recv_sem=rr, device_id=who,
            device_id_type=MESH)

    row_copies = []
    for k, p in enumerate(steps):
        row_copies.append(send(
            y2_ref.at[lays[k // 2], pl.ds((k % 2) * 128, 128), :], rx.at[k],
            s_row.at[k], r_row.at[k], at(*p, c)))
    for copy in row_copies:
        copy.start()

    def heads(ns):
        grams = []
        norms = []
        for n in ns:
            v = y1_ref[n]
            g = lax.dot_general(v, v, (((1,), (1,)), ((), ())), preferred_element_type=f32)
            norm = jnp.sqrt(trace(g)) + norm_epsilon
            grams.append(g * (1.0 / (norm * norm)))
            norms.append(norm)
        for n, q, norm in zip(ns, polynomials(grams, mm), norms):
            high, low = split(q * (math.sqrt(max(ROWS, LATENT)) / norm))
            q1_ref[n, 0] = high
            q1_ref[n, 1] = low

    heads((0, 1))
    for copy in row_copies:
        copy.wait()

    def gram_rows(i):
        total = None
        for v in [y2_ref.at[lay]] + [rx.at[k] for k in range(6)]:
            left = v[:, pl.ds(i * T, T)]
            right = v[:, pl.ds(i * T, LATENT - i * T)]
            g = lax.dot_general(left, right, (((0,), (0,)), ((), ())), preferred_element_type=f32)
            total = g if total is None else total + g
        return total

    for i4 in range(4):
        g = gram_rows(i4)
        for j4 in range(i4, 4):
            b = BLOCKS.index((i4, j4))
            part[pl.ds(b * T, T), :] = g[:, (j4 - i4) * T:(j4 - i4 + 1) * T]

    theirs = pl.ds(pl.multiple_of((1 - c) * HALF, 8), HALF)
    mine = pl.ds(pl.multiple_of(c * HALF, 8), HALF)
    swap = send(part.at[theirs, :], core_in, s_core, r_core, partner)
    swap.start()
    swap.wait()
    own[...] = part[mine, :] + core_in[...]

    rs_copies = []
    for k, (p, t2) in enumerate(team):
        rs_copies.append(send(
            own.at[pl.ds(pl.multiple_of(t2 * PIECE, 8), PIECE), :], rs.at[k],
            s_rs.at[k], r_rs.at[k], at(*p, c)))
    for copy in rs_copies:
        copy.start()
    heads((2, 3))
    for copy in rs_copies:
        copy.wait()
    total = own[pl.ds(pl.multiple_of(t * PIECE, 8), PIECE), :]
    for k in range(15):
        total = total + rs[k]
    here = pl.ds(pl.multiple_of(c * HALF + t * PIECE, 8), PIECE)
    gath[here, :] = total
    ag_copies = [
        send(gath.at[here, :], gath.at[here, :], s_ag.at[k], r_ag.at[k], at(*p, c))
        for k, (p, _) in enumerate(team)
    ]
    for copy in ag_copies:
        copy.start()
    for copy in ag_copies:
        copy.wait_send()
    for k in range(15):
        di, dj, dz = OFFSETS[k]
        t3 = (((i + di) % 2) * 2 + (j + dj) % 2) * 4 + (z + 4 - dz) % 4
        there = pl.ds(pl.multiple_of(c * HALF + t3 * PIECE, 8), PIECE)
        send(gath.at[there, :], gath.at[there, :], s_ag.at[k], r_ag.at[k],
             at(*team[k][0], c)).wait_recv()
    relay = send(gath.at[mine, :], gath.at[mine, :], s_rel, r_rel, partner)
    relay.start()
    relay.wait_send()
    send(gath.at[theirs, :], gath.at[theirs, :], s_rel, r_rel, partner).wait_recv()

    tiles = {}
    for b, (bi, bj) in enumerate(BLOCKS):
        v = gath[pl.ds(b * T, T), :]
        tiles[bi, bj] = v
        if bi != bj:
            tiles[bj, bi] = v.T
    gram = jnp.concatenate(
        [jnp.concatenate([tiles[r, k] for k in range(4)], 1) for r in range(4)], 0)
    norm = jnp.sqrt(trace(gram)) + norm_epsilon
    q = polynomials([gram * (1.0 / (norm * norm))], mm_even)[0]
    parts = split(q * (math.sqrt(ALL_ROWS) / norm))
    for k in range(2):
        q2_ref[lay, k] = parts[k]
        packed[k, 0:256, :] = parts[k][0:256, :]
        packed[k, 256:384, 0:256] = parts[k][256:384, 256:512]
        packed[k, 256:384, 256:512] = parts[k][384:512, 256:512]
    q_copies = []
    for k, p in enumerate(steps):
        rows = pl.ds(pl.multiple_of((k % 2) * 192 + c * 96, 16), 96)
        for d in range(2):
            q_copies.append(send(
                packed.at[:, rows, :], rxq.at[k // 2, :, rows, :], s_q.at[k, d],
                r_q.at[k, c], at(*p, d)))
    for copy in q_copies:
        copy.start()
    for copy in q_copies:
        copy.wait_send()
    for k, p in enumerate(steps):
        for d in range(2):
            rows = pl.ds((k % 2) * 192 + d * 96, 96)
            send(packed.at[:, rows, :], rxq.at[k // 2, :, rows, :], s_q.at[k, d],
                 r_q.at[k, d], at(*p, d)).wait_recv()
    for a in range(3):
        for k in range(2):
            top = rxq[a, k, 0:256, :]
            q2_ref[lays[a], k, 0:256, :] = top
            q2_ref[lays[a], k, 256:512, 0:256] = top[:, 256:512].T
            q2_ref[lays[a], k, 256:384, 256:512] = rxq[a, k, 256:384, 0:256]
            q2_ref[lays[a], k, 384:512, 256:512] = rxq[a, k, 256:384, 256:512]


def finish(y1_ref, y2_ref, q1_ref, q2_ref, o1_ref, o2_ref):
    v = y1_ref[0]
    o1_ref[0] = dot(q1_ref[0, 0], v) + dot(q1_ref[0, 1], v)
    w = y2_ref[0]
    o2_ref[0] = dot(w, q2_ref[0, 0]) + dot(w, q2_ref[0, 1])


def shards(momentum, grad_one, grad_two):
    vmem = pl.BlockSpec(memory_space=pltpu.VMEM)
    dma = pltpu.SemaphoreType.DMA
    y1, y2, q1, q2 = pl.pallas_call(
        exchange,
        out_shape=(
            jax.ShapeDtypeStruct((LAYERS, ROWS, LATENT), bf16),
            jax.ShapeDtypeStruct((LAYERS, ROWS, LATENT), bf16),
            jax.ShapeDtypeStruct((LAYERS, 2, ROWS, ROWS), bf16),
            jax.ShapeDtypeStruct((LAYERS, 2, LATENT, LATENT), bf16),
        ),
        in_specs=[vmem] * 3,
        out_specs=(vmem,) * 4,
        scratch_shapes=[
            pltpu.VMEM((6, 128, LATENT), bf16),
            pltpu.VMEM((2 * HALF, T), f32),
            pltpu.VMEM((HALF, T), f32),
            pltpu.VMEM((HALF, T), f32),
            pltpu.VMEM((15, PIECE, T), f32),
            pltpu.VMEM((2 * HALF, T), f32),
            pltpu.VMEM((2, 384, LATENT), bf16),
            pltpu.VMEM((3, 2, 384, LATENT), bf16),
            dma((6,)), dma((6,)), dma, dma, dma((15,)), dma((15,)), dma((15,)), dma((15,)),
            dma, dma, dma((6, 2)), dma((6, 2)),
        ],
        compiler_params=pltpu.CompilerParams(
            collective_id=0, has_side_effects=True, vmem_limit_bytes=56 << 20),
        name="exchange",
    )(momentum, grad_one, grad_two)

    def block(*shape):
        return pl.BlockSpec((1, *shape), lambda n: (n,) + (0,) * len(shape))

    return pl.pallas_call(
        finish,
        grid=(LAYERS,),
        out_shape=(jax.ShapeDtypeStruct((LAYERS, ROWS, LATENT), f32),) * 2,
        in_specs=[block(ROWS, LATENT), block(ROWS, LATENT), block(2, ROWS, ROWS),
                  block(2, LATENT, LATENT)],
        out_specs=(block(ROWS, LATENT),) * 2,
        name="finish",
    )(y1, y2, q1, q2)


def solution(mesh):
    spec = P(None, ("layer", "head"), None)
    return jax.shard_map(
        shards, mesh=mesh, in_specs=(spec,) * 3, out_specs=(spec,) * 2, check_vma=False
    )
```

```python
import functools
import math

import jax
import jax.numpy as jnp
from jax import lax
from jax.experimental import pallas as pl
from jax.experimental.pallas import tpu as pltpu
from jax.sharding import PartitionSpec as P

NS_ITERS = 5
quintic_a = 3.4445
quintic_b = -4.775
quintic_c = 2.0315
norm_epsilon = 1e-07
momentum_decay = 0.95

bf16 = jnp.bfloat16
f32 = jnp.float32
MESH = pl.DeviceIdType.MESH
LAYERS, ROWS, LATENT = 4, 256, 512
ALL_ROWS = 32768
T = 128
BLOCKS = [(i, j) for i in range(4) for j in range(i, 4)]
HALF = len(BLOCKS) * T // 2
PIECE = HALF // 16
QUARTER = HALF // 2
SHARES = 2
SHARE = QUARTER // SHARES
OFFSETS = [(1, 1, 2), (1, 1, 0), (1, 0, 2), (0, 1, 2)]
OFFSETS += [(i, j, z) for z in (1, 3) for i in (0, 1) for j in (0, 1)]
OFFSETS += [(1, 0, 0), (0, 1, 0), (0, 0, 2)]


def split(x):
    high = x.astype(bf16)
    return high, (x - high.astype(f32)).astype(bf16)


def dot(x, y):
    return jnp.dot(x, y, preferred_element_type=f32)


def dot3(x, y):
    return dot(x[0], y[0]) + (dot(x[0], y[1]) + dot(x[1], y[0]))


def mm(x, y):
    return dot3(x, y)


def mm_even(x, y):
    h = x[0].shape[0] // 2
    top = dot3([t[:h] for t in x], y)
    low = dot3([t[h:] for t in x], [t[:, h:] for t in y])
    return jnp.concatenate([top, jnp.concatenate([top[:, h:].T, low], 1)], 0)


def eye(n):
    rows = lax.broadcasted_iota(jnp.int32, (n, n), 0)
    return rows == lax.broadcasted_iota(jnp.int32, (n, n), 1)


def polynomials(grams, product):
    n = grams[0].shape[0]
    diag = jnp.where(eye(n), f32(quintic_a), f32(0.0))
    s, q = list(grams), [None] * len(grams)
    for k in range(NS_ITERS):
        parts = [split(t) for t in s]
        m = [
            diag + (quintic_b * t + quintic_c * product(u, u)) for t, u in zip(s, parts)
        ]
        ms = [split(t) for t in m]
        if k < NS_ITERS - 1:
            r = [split(product(u, v)) for u, v in zip(parts, ms)]
            s = [product(u, v) for u, v in zip(r, ms)]
        q = m if k == 0 else [product(split(u), v) for u, v in zip(q, ms)]
    return q


def unpacked(blocks):
    tiles = {}
    for b, (i, j) in enumerate(BLOCKS):
        v = blocks[b * T:(b + 1) * T, :]
        tiles[i, j] = v
        if i != j:
            tiles[j, i] = v.T
    return jnp.concatenate(
        [jnp.concatenate([tiles[i, j] for j in range(4)], 1) for i in range(4)], 0)


def trace(x):
    return jnp.sum(jnp.where(eye(x.shape[0]), x, f32(0.0)))


def exchange(
    m_hbm, g1_hbm, g2_hbm, o1_ref, o2_ref,
    ins, y1_ref, y2_ref, q1_ref, rx, part, core_in, own, rs, gath, packed, rxq,
    s_in, s_row, r_row, s_core, r_core, s_rs, r_rs, s_ag, r_ag, s_rel, r_rel,
    s_q, r_q, s_qr, r_qr,
):
    x = lax.axis_index("layer")
    head = lax.axis_index("head")
    y, z, c = head // 8, (head // 2) % 4, head % 2
    b0, b1 = (x + z) % 2, (y + z) % 2
    lay = b0 + 2 * b1
    lays = [(1 - b0) + 2 * b1, b0 + 2 * (1 - b1), (1 - b0) + 2 * (1 - b1)]
    i, j = x // 2, y // 2
    t = (i * 2 + j) * 4 + z

    def at(x, y, z, c):
        return (x, (y * 4 + z) * 2 + c)

    steps = []
    for a in range(3):
        for s in range(2):
            d = 1 if s == 0 else 3
            steps.append(((x + d) % 4 if a == 0 else x, (y + d) % 4 if a == 1 else y,
                          (z + d) % 4 if a == 2 else z))
    team = []
    for di, dj, dz in OFFSETS:
        i2, j2, z2 = (i + di) % 2, (j + dj) % 2, (z + dz) % 4
        team.append(((2 * i2 + (b0 + z2) % 2, 2 * j2 + (b1 + z2) % 2, z2),
                     (i2 * 2 + j2) * 4 + z2))
    partner = at(x, y, z, 1 - c)

    loads = [
        [pltpu.make_async_copy(h.at[n], ins.at[k, n], s_in.at[k, n])
         for k, h in enumerate((m_hbm, g1_hbm, g2_hbm))]
        for n in range(LAYERS)
    ]
    for group in loads:
        for copy in group:
            copy.start()
    barrier = pltpu.get_barrier_semaphore()
    greet = [partner]
    greet += [at(*p, c) for p in steps]
    greet += [at(*p, c) for p, _ in team]
    for who in greet:
        pl.semaphore_signal(barrier, inc=1, device_id=who, device_id_type=MESH)

    for n in range(LAYERS):
        for copy in loads[n]:
            copy.wait()
        one = (momentum_decay * ins[0, n].astype(f32) + ins[1, n].astype(f32)).astype(bf16)
        y1_ref[n] = one
        y2_ref[n] = (momentum_decay * one.astype(f32) + ins[2, n].astype(f32)).astype(bf16)

    pl.semaphore_wait(barrier, len(greet))

    def send(src, dst, ss, rr, who):
        return pltpu.make_async_remote_copy(
            src_ref=src, dst_ref=dst, send_sem=ss, recv_sem=rr, device_id=who,
            device_id_type=MESH)

    row_copies = []
    for k, p in enumerate(steps):
        row_copies.append(send(
            y2_ref.at[lays[k // 2], pl.ds((k % 2) * 128, 128), :], rx.at[k],
            s_row.at[k], r_row.at[k], at(*p, c)))
    for copy in row_copies:
        copy.start()

    def heads(ns):
        grams = []
        norms = []
        for n in ns:
            v = y1_ref[n]
            g = lax.dot_general(v, v, (((1,), (1,)), ((), ())), preferred_element_type=f32)
            norm = jnp.sqrt(trace(g)) + norm_epsilon
            grams.append(g * (1.0 / (norm * norm)))
            norms.append(norm)
        for n, q, norm in zip(ns, polynomials(grams, mm), norms):
            high, low = split(q * (math.sqrt(max(ROWS, LATENT)) / norm))
            q1_ref[n, 0] = high
            q1_ref[n, 1] = low

    for copy in row_copies:
        copy.wait()

    def gram_rows(i):
        total = None
        for v in [y2_ref.at[lay]] + [rx.at[k] for k in range(6)]:
            left = v[:, pl.ds(i * T, T)]
            right = v[:, pl.ds(i * T, LATENT - i * T)]
            g = lax.dot_general(left, right, (((0,), (0,)), ((), ())), preferred_element_type=f32)
            total = g if total is None else total + g
        return total

    for i4 in range(4):
        g = gram_rows(i4)
        for j4 in range(i4, 4):
            b = BLOCKS.index((i4, j4))
            part[pl.ds(b * T, T), :] = g[:, (j4 - i4) * T:(j4 - i4 + 1) * T]

    theirs = pl.ds(pl.multiple_of((1 - c) * HALF, 8), HALF)
    mine = pl.ds(pl.multiple_of(c * HALF, 8), HALF)
    swap = send(part.at[theirs, :], core_in, s_core, r_core, partner)
    swap.start()
    swap.wait()
    own[...] = part[mine, :] + core_in[...]

    rs_copies = []
    for k, (p, t2) in enumerate(team):
        rs_copies.append(send(
            own.at[pl.ds(pl.multiple_of(t2 * PIECE, 8), PIECE), :], rs.at[k],
            s_rs.at[k], r_rs.at[k], at(*p, c)))
    for copy in rs_copies:
        copy.start()
    heads((0, 1))
    for copy in rs_copies:
        copy.wait()
    total = own[pl.ds(pl.multiple_of(t * PIECE, 8), PIECE), :]
    for k in range(15):
        total = total + rs[k]
    here = pl.ds(pl.multiple_of(c * HALF + t * PIECE, 8), PIECE)
    gath[here, :] = total
    ag_copies = [
        send(gath.at[here, :], gath.at[here, :], s_ag.at[k], r_ag.at[k], at(*p, c))
        for k, (p, _) in enumerate(team)
    ]
    for copy in ag_copies:
        copy.start()
    heads((2, 3))

    def relay(k, t3, core):
        there = pl.ds(pl.multiple_of(core * HALF + t3 * PIECE, 8), PIECE)
        return send(gath.at[there, :], gath.at[there, :], s_rel.at[k], r_rel.at[k], partner)

    relays = [(15, t)]
    for k, (di, dj, dz) in enumerate(OFFSETS):
        relays.append((k, (((i + di) % 2) * 2 + (j + dj) % 2) * 4 + (z + 4 - dz) % 4))
    for k, t3 in [relays[0]] + relays[:0:-1]:
        if k < 15:
            there = pl.ds(pl.multiple_of(c * HALF + t3 * PIECE, 8), PIECE)
            send(gath.at[there, :], gath.at[there, :], s_ag.at[k], r_ag.at[k],
                 at(*team[k][0], c)).wait_recv()
        relay(k, t3, c).start()
    for copy in ag_copies:
        copy.wait_send()
    for k, t3 in relays:
        relay(k, t3, c).wait_send()
    for k, t3 in relays:
        relay(k, t3, 1 - c).wait_recv()

    gram = unpacked(gath[...])
    norm = jnp.sqrt(trace(gram)) + norm_epsilon
    q = polynomials([gram * (1.0 / (norm * norm))], mm_even)[0]
    parts = split(q * (math.sqrt(ALL_ROWS) / norm))
    for k in range(2):
        for b, (bi, bj) in enumerate(BLOCKS):
            packed[k, b * T:(b + 1) * T, :] = parts[k][bi * T:(bi + 1) * T, bj * T:(bj + 1) * T]

    def part_of(a, s, h, core, src, ss, rr, who):
        rows = pl.ds(pl.multiple_of((s * 2 + core) * QUARTER + h * SHARE, 16), SHARE)
        return send(src.at[:, rows, :], rxq.at[a, :, rows, :], ss.at[a, s, h], rr.at[a, s, h], who)

    order = [(a, s, h) for h in range(SHARES) for a in range(3) for s in range(2)]
    q_copies = [
        part_of(a, s, h, c, packed, s_q, r_q, at(*steps[2 * a + s], c)) for a, s, h in order
    ]
    for copy in q_copies:
        copy.start()
    w = y2_ref[lay]
    o2_ref[lay] = dot(w, parts[0]) + dot(w, parts[1])
    for n in range(LAYERS):
        v = y1_ref[n]
        o1_ref[n] = dot(q1_ref[n, 0], v) + dot(q1_ref[n, 1], v)
    passed = []
    for copy, (a, s, h) in zip(q_copies, order):
        copy.wait()
        passed.append(part_of(a, s, h, c, rxq.at[a], s_qr, r_qr, partner))
        passed[-1].start()
    for copy in passed:
        copy.wait_send()
    for a in range(3):
        for s in range(2):
            for h in range(SHARES):
                part_of(a, s, h, 1 - c, rxq.at[a], s_qr, r_qr, partner).wait_recv()
        w = y2_ref[lays[a]]
        total = None
        for k in range(2):
            full = unpacked(rxq[a, k])
            term = dot(w, full)
            total = term if total is None else total + term
        o2_ref[lays[a]] = total


def shards(momentum, grad_one, grad_two):
    vmem = pl.BlockSpec(memory_space=pltpu.VMEM)
    hbm = pl.BlockSpec(memory_space=pltpu.MemorySpace.HBM)
    dma = pltpu.SemaphoreType.DMA
    return pl.pallas_call(
        exchange,
        out_shape=(jax.ShapeDtypeStruct((LAYERS, ROWS, LATENT), f32),) * 2,
        in_specs=[hbm] * 3,
        out_specs=(vmem,) * 2,
        scratch_shapes=[
            pltpu.VMEM((3, LAYERS, ROWS, LATENT), bf16),
            pltpu.VMEM((LAYERS, ROWS, LATENT), bf16),
            pltpu.VMEM((LAYERS, ROWS, LATENT), bf16),
            pltpu.VMEM((LAYERS, 2, ROWS, ROWS), bf16),
            pltpu.VMEM((6, 128, LATENT), bf16),
            pltpu.VMEM((2 * HALF, T), f32),
            pltpu.VMEM((HALF, T), f32),
            pltpu.VMEM((HALF, T), f32),
            pltpu.VMEM((15, PIECE, T), f32),
            pltpu.VMEM((2 * HALF, T), f32),
            pltpu.VMEM((2, 2 * HALF, T), bf16),
            pltpu.VMEM((3, 2, 2 * HALF, T), bf16),
            dma((3, LAYERS)), dma((6,)), dma((6,)), dma, dma,
            dma((15,)), dma((15,)), dma((15,)), dma((15,)), dma((16,)), dma((16,)),
            dma((3, 2, SHARES)), dma((3, 2, SHARES)), dma((3, 2, SHARES)), dma((3, 2, SHARES)),
        ],
        compiler_params=pltpu.CompilerParams(
            collective_id=0, has_side_effects=True, vmem_limit_bytes=59 << 20),
        name="exchange",
    )(momentum, grad_one, grad_two)


def solution(mesh):
    spec = P(None, ("layer", "head"), None)
    return jax.shard_map(
        shards, mesh=mesh, in_specs=(spec,) * 3, out_specs=(spec,) * 2, check_vma=False
    )
```

```python
import functools
import math

import jax
import jax.numpy as jnp
from jax import lax
from jax.experimental import pallas as pl
from jax.experimental.pallas import tpu as pltpu
from jax.sharding import PartitionSpec as P

NS_ITERS = 5
quintic_a = 3.4445
quintic_b = -4.775
quintic_c = 2.0315
norm_epsilon = 1e-07
momentum_decay = 0.95

bf16 = jnp.bfloat16
f32 = jnp.float32
MESH = pl.DeviceIdType.MESH
LAYERS, ROWS, LATENT = 4, 256, 512
ALL_ROWS = 32768
T = 128
BLOCKS = [(i, j) for i in range(4) for j in range(i, 4)]
HALF = len(BLOCKS) * T // 2
PIECE = HALF // 16
QUARTER = HALF // 2
SHARES = 2
SHARE = QUARTER // SHARES
OFFSETS = [(1, 1, 2), (1, 1, 0), (1, 0, 2), (0, 1, 2)]
OFFSETS += [(i, j, z) for z in (1, 3) for i in (0, 1) for j in (0, 1)]
OFFSETS += [(1, 0, 0), (0, 1, 0), (0, 0, 2)]


def split(x):
    high = x.astype(bf16)
    return high, (x - high.astype(f32)).astype(bf16)


def dot(x, y):
    return jnp.dot(x, y, preferred_element_type=f32)


def dot3(x, y):
    return dot(x[0], y[0]) + (dot(x[0], y[1]) + dot(x[1], y[0]))


def mm(x, y):
    return dot3(x, y)


def mm_even(x, y):
    h = x[0].shape[0] // 2
    top = dot3([t[:h] for t in x], y)
    low = dot3([t[h:] for t in x], [t[:, h:] for t in y])
    return jnp.concatenate([top, jnp.concatenate([top[:, h:].T, low], 1)], 0)


def eye(n):
    rows = lax.broadcasted_iota(jnp.int32, (n, n), 0)
    return rows == lax.broadcasted_iota(jnp.int32, (n, n), 1)


def polynomials(grams, product):
    n = grams[0].shape[0]
    diag = jnp.where(eye(n), f32(quintic_a), f32(0.0))
    s, q = list(grams), [None] * len(grams)
    for k in range(NS_ITERS):
        parts = [split(t) for t in s]
        m = [
            diag + (quintic_b * t + quintic_c * product(u, u)) for t, u in zip(s, parts)
        ]
        ms = [split(t) for t in m]
        if k < NS_ITERS - 1:
            r = [split(product(u, v)) for u, v in zip(parts, ms)]
            s = [product(u, v) for u, v in zip(r, ms)]
        q = m if k == 0 else [product(split(u), v) for u, v in zip(q, ms)]
    return q


def unpacked(blocks):
    tiles = {}
    for b, (i, j) in enumerate(BLOCKS):
        v = blocks[b * T:(b + 1) * T, :]
        tiles[i, j] = v
        if i != j:
            tiles[j, i] = v.T
    return jnp.concatenate(
        [jnp.concatenate([tiles[i, j] for j in range(4)], 1) for i in range(4)], 0)


def trace(x):
    return jnp.sum(jnp.where(eye(x.shape[0]), x, f32(0.0)))


def exchange(
    m_hbm, g1_hbm, g2_hbm, o1_ref, own2_ref, y2_ref, rxq,
    ins, y1_ref, q1_ref, rx, part, core_in, own, rs, gath, packed,
    s_in, s_row, r_row, s_core, r_core, s_rs, r_rs, s_ag, r_ag, s_rel, r_rel,
    s_q, r_q, s_qr, r_qr,
):
    x = lax.axis_index("layer")
    head = lax.axis_index("head")
    y, z, c = head // 8, (head // 2) % 4, head % 2
    b0, b1 = (x + z) % 2, (y + z) % 2
    lay = b0 + 2 * b1
    lays = [(1 - b0) + 2 * b1, b0 + 2 * (1 - b1), (1 - b0) + 2 * (1 - b1)]
    i, j = x // 2, y // 2
    t = (i * 2 + j) * 4 + z

    def at(x, y, z, c):
        return (x, (y * 4 + z) * 2 + c)

    steps = []
    for a in range(3):
        for s in range(2):
            d = 1 if s == 0 else 3
            steps.append(((x + d) % 4 if a == 0 else x, (y + d) % 4 if a == 1 else y,
                          (z + d) % 4 if a == 2 else z))
    team = []
    for di, dj, dz in OFFSETS:
        i2, j2, z2 = (i + di) % 2, (j + dj) % 2, (z + dz) % 4
        team.append(((2 * i2 + (b0 + z2) % 2, 2 * j2 + (b1 + z2) % 2, z2),
                     (i2 * 2 + j2) * 4 + z2))
    partner = at(x, y, z, 1 - c)

    loads = [
        [pltpu.make_async_copy(h.at[n], ins.at[k, n], s_in.at[k, n])
         for k, h in enumerate((m_hbm, g1_hbm, g2_hbm))]
        for n in range(LAYERS)
    ]
    for group in loads:
        for copy in group:
            copy.start()
    barrier = pltpu.get_barrier_semaphore()
    greet = [partner]
    greet += [at(*p, c) for p in steps]
    greet += [at(*p, c) for p, _ in team]
    for who in greet:
        pl.semaphore_signal(barrier, inc=1, device_id=who, device_id_type=MESH)

    for n in range(LAYERS):
        for copy in loads[n]:
            copy.wait()
        one = (momentum_decay * ins[0, n].astype(f32) + ins[1, n].astype(f32)).astype(bf16)
        y1_ref[n] = one
        y2_ref[n] = (momentum_decay * one.astype(f32) + ins[2, n].astype(f32)).astype(bf16)

    pl.semaphore_wait(barrier, len(greet))

    def send(src, dst, ss, rr, who):
        return pltpu.make_async_remote_copy(
            src_ref=src, dst_ref=dst, send_sem=ss, recv_sem=rr, device_id=who,
            device_id_type=MESH)

    row_copies = []
    for k, p in enumerate(steps):
        row_copies.append(send(
            y2_ref.at[lays[k // 2], pl.ds((k % 2) * 128, 128), :], rx.at[k],
            s_row.at[k], r_row.at[k], at(*p, c)))
    for copy in row_copies:
        copy.start()

    def heads(ns):
        grams = []
        norms = []
        for n in ns:
            v = y1_ref[n]
            g = lax.dot_general(v, v, (((1,), (1,)), ((), ())), preferred_element_type=f32)
            norm = jnp.sqrt(trace(g)) + norm_epsilon
            grams.append(g * (1.0 / (norm * norm)))
            norms.append(norm)
        for n, q, norm in zip(ns, polynomials(grams, mm), norms):
            high, low = split(q * (math.sqrt(max(ROWS, LATENT)) / norm))
            q1_ref[n, 0] = high
            q1_ref[n, 1] = low

    for copy in row_copies:
        copy.wait()

    def gram_rows(i):
        total = None
        for v in [y2_ref.at[lay]] + [rx.at[k] for k in range(6)]:
            left = v[:, pl.ds(i * T, T)]
            right = v[:, pl.ds(i * T, LATENT - i * T)]
            g = lax.dot_general(left, right, (((0,), (0,)), ((), ())), preferred_element_type=f32)
            total = g if total is None else total + g
        return total

    for i4 in range(4):
        g = gram_rows(i4)
        for j4 in range(i4, 4):
            b = BLOCKS.index((i4, j4))
            part[pl.ds(b * T, T), :] = g[:, (j4 - i4) * T:(j4 - i4 + 1) * T]

    theirs = pl.ds(pl.multiple_of((1 - c) * HALF, 8), HALF)
    mine = pl.ds(pl.multiple_of(c * HALF, 8), HALF)
    swap = send(part.at[theirs, :], core_in, s_core, r_core, partner)
    swap.start()
    swap.wait()
    own[...] = part[mine, :] + core_in[...]

    rs_copies = []
    for k, (p, t2) in enumerate(team):
        rs_copies.append(send(
            own.at[pl.ds(pl.multiple_of(t2 * PIECE, 8), PIECE), :], rs.at[k],
            s_rs.at[k], r_rs.at[k], at(*p, c)))
    for copy in rs_copies:
        copy.start()
    heads((0, 1))
    for copy in rs_copies:
        copy.wait()
    total = own[pl.ds(pl.multiple_of(t * PIECE, 8), PIECE), :]
    for k in range(15):
        total = total + rs[k]
    here = pl.ds(pl.multiple_of(c * HALF + t * PIECE, 8), PIECE)
    gath[here, :] = total
    ag_copies = [
        send(gath.at[here, :], gath.at[here, :], s_ag.at[k], r_ag.at[k], at(*p, c))
        for k, (p, _) in enumerate(team)
    ]
    for copy in ag_copies:
        copy.start()
    heads((2, 3))

    def relay(k, t3, core):
        there = pl.ds(pl.multiple_of(core * HALF + t3 * PIECE, 8), PIECE)
        return send(gath.at[there, :], gath.at[there, :], s_rel.at[k], r_rel.at[k], partner)

    relays = [(15, t)]
    for k, (di, dj, dz) in enumerate(OFFSETS):
        relays.append((k, (((i + di) % 2) * 2 + (j + dj) % 2) * 4 + (z + 4 - dz) % 4))
    for k, t3 in [relays[0]] + relays[:0:-1]:
        if k < 15:
            there = pl.ds(pl.multiple_of(c * HALF + t3 * PIECE, 8), PIECE)
            send(gath.at[there, :], gath.at[there, :], s_ag.at[k], r_ag.at[k],
                 at(*team[k][0], c)).wait_recv()
        relay(k, t3, c).start()
    for copy in ag_copies:
        copy.wait_send()
    for k, t3 in relays:
        relay(k, t3, c).wait_send()
    for k, t3 in relays:
        relay(k, t3, 1 - c).wait_recv()

    gram = unpacked(gath[...])
    norm = jnp.sqrt(trace(gram)) + norm_epsilon
    q = polynomials([gram * (1.0 / (norm * norm))], mm_even)[0]
    parts = split(q * (math.sqrt(ALL_ROWS) / norm))
    for k in range(2):
        for b, (bi, bj) in enumerate(BLOCKS):
            packed[k, b * T:(b + 1) * T, :] = parts[k][bi * T:(bi + 1) * T, bj * T:(bj + 1) * T]

    def part_of(a, s, h, core, src, ss, rr, who):
        rows = pl.ds(pl.multiple_of((s * 2 + core) * QUARTER + h * SHARE, 16), SHARE)
        return send(src.at[:, rows, :], rxq.at[a, :, rows, :], ss.at[a, s, h], rr.at[a, s, h], who)

    order = [(a, s, h) for h in range(SHARES) for a in range(3) for s in range(2)]
    q_copies = [
        part_of(a, s, h, c, packed, s_q, r_q, at(*steps[2 * a + s], c)) for a, s, h in order
    ]
    for copy in q_copies:
        copy.start()
    w = y2_ref[lay]
    own2_ref[...] = dot(w, parts[0]) + dot(w, parts[1])
    for n in range(LAYERS):
        v = y1_ref[n]
        o1_ref[n] = dot(q1_ref[n, 0], v) + dot(q1_ref[n, 1], v)
    passed = []
    for copy, (a, s, h) in zip(q_copies, order):
        copy.wait()
        passed.append(part_of(a, s, h, c, rxq.at[a], s_qr, r_qr, partner))
        passed[-1].start()
    for copy in passed:
        copy.wait_send()
    for a, s, h in order:
        part_of(a, s, h, 1 - c, rxq.at[a], s_qr, r_qr, partner).wait_recv()


def finish(o1_ref, own2_ref, y2_ref, rxq, out1, out2, buf, sems):
    x = lax.axis_index("layer")
    head = lax.axis_index("head")
    y, z = head // 8, (head // 2) % 4
    b0, b1 = (x + z) % 2, (y + z) % 2
    copies = [pltpu.make_async_copy(
        own2_ref, out2.at[b0 + 2 * b1], sems.at[LAYERS])]
    for n in range(LAYERS):
        copies.append(pltpu.make_async_copy(o1_ref.at[n], out1.at[n], sems.at[n]))
    for copy in copies:
        copy.start()
    lays = [(1 - b0) + 2 * b1, b0 + 2 * (1 - b1), (1 - b0) + 2 * (1 - b1)]
    for a in range(3):
        w = y2_ref[lays[a]]
        buf[a] = dot(w, unpacked(rxq[a, 0])) + dot(w, unpacked(rxq[a, 1]))
        copies.append(pltpu.make_async_copy(buf.at[a], out2.at[lays[a]], sems.at[LAYERS + 1 + a]))
        copies[-1].start()
    for copy in copies:
        copy.wait()


def shards(momentum, grad_one, grad_two):
    vmem = pl.BlockSpec(memory_space=pltpu.VMEM)
    hbm = pl.BlockSpec(memory_space=pltpu.MemorySpace.HBM)
    dma = pltpu.SemaphoreType.DMA
    given = pl.pallas_call(
        exchange,
        out_shape=(
            jax.ShapeDtypeStruct((LAYERS, ROWS, LATENT), f32),
            jax.ShapeDtypeStruct((ROWS, LATENT), f32),
            jax.ShapeDtypeStruct((LAYERS, ROWS, LATENT), bf16),
            jax.ShapeDtypeStruct((3, 2, 2 * HALF, T), bf16),
        ),
        in_specs=[hbm] * 3,
        out_specs=(vmem,) * 4,
        scratch_shapes=[
            pltpu.VMEM((3, LAYERS, ROWS, LATENT), bf16),
            pltpu.VMEM((LAYERS, ROWS, LATENT), bf16),
            pltpu.VMEM((LAYERS, 2, ROWS, ROWS), bf16),
            pltpu.VMEM((6, 128, LATENT), bf16),
            pltpu.VMEM((2 * HALF, T), f32),
            pltpu.VMEM((HALF, T), f32),
            pltpu.VMEM((HALF, T), f32),
            pltpu.VMEM((15, PIECE, T), f32),
            pltpu.VMEM((2 * HALF, T), f32),
            pltpu.VMEM((2, 2 * HALF, T), bf16),
            dma((3, LAYERS)), dma((6,)), dma((6,)), dma, dma,
            dma((15,)), dma((15,)), dma((15,)), dma((15,)), dma((16,)), dma((16,)),
            dma((3, 2, SHARES)), dma((3, 2, SHARES)), dma((3, 2, SHARES)), dma((3, 2, SHARES)),
        ],
        compiler_params=pltpu.CompilerParams(
            collective_id=0, has_side_effects=True, vmem_limit_bytes=32 << 20),
        name="exchange",
    )(*[
        pltpu.with_memory_space_constraint(v, pltpu.MemorySpace.HBM)
        for v in (momentum, grad_one, grad_two)
    ])
    return pl.pallas_call(
        finish,
        out_shape=(jax.ShapeDtypeStruct((LAYERS, ROWS, LATENT), f32),) * 2,
        in_specs=[vmem] * 4,
        out_specs=(hbm,) * 2,
        scratch_shapes=[pltpu.VMEM((3, ROWS, LATENT), f32), dma((LAYERS + 4,))],
        compiler_params=pltpu.CompilerParams(vmem_limit_bytes=12 << 20),
        name="finish",
    )(*given)


def solution(mesh):
    spec = P(None, ("layer", "head"), None)
    return jax.shard_map(
        shards, mesh=mesh, in_specs=(spec,) * 3, out_specs=(spec,) * 2, check_vma=False
    )
```

```python
import functools
import math

import jax
import jax.numpy as jnp
from jax import lax
from jax.experimental import pallas as pl
from jax.experimental.pallas import tpu as pltpu
from jax.sharding import PartitionSpec as P

NS_ITERS = 5
quintic_a = 3.4445
quintic_b = -4.775
quintic_c = 2.0315
norm_epsilon = 1e-07
momentum_decay = 0.95

bf16 = jnp.bfloat16
f32 = jnp.float32
MESH = pl.DeviceIdType.MESH
LAYERS, ROWS, LATENT = 4, 256, 512
ALL_ROWS = 32768
T = 128
BLOCKS = [(i, j) for i in range(4) for j in range(i, 4)]
HALF = len(BLOCKS) * T // 2
PIECE = HALF // 16
QUARTER = HALF // 2
SHARES = 2
SHARE = QUARTER // SHARES
OFFSETS = [(1, 1, 2), (1, 1, 0), (1, 0, 2), (0, 1, 2)]
OFFSETS += [(i, j, z) for z in (1, 3) for i in (0, 1) for j in (0, 1)]
OFFSETS += [(1, 0, 0), (0, 1, 0), (0, 0, 2)]


def split(x):
    high = x.astype(bf16)
    return high, (x - high.astype(f32)).astype(bf16)


def dot(x, y):
    return jnp.dot(x, y, preferred_element_type=f32)


def dot3(x, y):
    return dot(x[0], y[0]) + (dot(x[0], y[1]) + dot(x[1], y[0]))


def mm(x, y):
    return dot3(x, y)


def mm_even(x, y):
    h = x[0].shape[0] // 2
    top = dot3([t[:h] for t in x], y)
    low = dot3([t[h:] for t in x], [t[:, h:] for t in y])
    return jnp.concatenate([top, jnp.concatenate([top[:, h:].T, low], 1)], 0)


def eye(n):
    rows = lax.broadcasted_iota(jnp.int32, (n, n), 0)
    return rows == lax.broadcasted_iota(jnp.int32, (n, n), 1)


def polynomials(grams, product):
    n = grams[0].shape[0]
    diag = jnp.where(eye(n), f32(quintic_a), f32(0.0))
    s, q = list(grams), [None] * len(grams)
    for k in range(NS_ITERS):
        parts = [split(t) for t in s]
        m = [
            diag + (quintic_b * t + quintic_c * product(u, u)) for t, u in zip(s, parts)
        ]
        ms = [split(t) for t in m]
        if k < NS_ITERS - 1:
            r = [split(product(u, v)) for u, v in zip(parts, ms)]
            s = [product(u, v) for u, v in zip(r, ms)]
        q = m if k == 0 else [product(split(u), v) for u, v in zip(q, ms)]
    return q


def unpacked(blocks):
    tiles = {}
    for b, (i, j) in enumerate(BLOCKS):
        v = blocks[b * T:(b + 1) * T, :]
        tiles[i, j] = v
        if i != j:
            tiles[j, i] = v.T
    return jnp.concatenate(
        [jnp.concatenate([tiles[i, j] for j in range(4)], 1) for i in range(4)], 0)


def trace(x):
    return jnp.sum(jnp.where(eye(x.shape[0]), x, f32(0.0)))


def exchange(
    m_hbm, g1_hbm, g2_hbm, o1_ref, own2_ref, y2_ref, rxq,
    ins, y1_ref, q1_ref, rx, part, core_in, own, rs, gath, packed, q2_ref,
    s_in, s_row, r_row, s_core, r_core, s_rs, r_rs, s_ag, r_ag, s_rel, r_rel,
    s_q, r_q, s_qr, r_qr,
):
    x = lax.axis_index("layer")
    head = lax.axis_index("head")
    y, z, c = head // 8, (head // 2) % 4, head % 2
    b0, b1 = (x + z) % 2, (y + z) % 2
    lay = b0 + 2 * b1
    lays = [(1 - b0) + 2 * b1, b0 + 2 * (1 - b1), (1 - b0) + 2 * (1 - b1)]
    i, j = x // 2, y // 2
    t = (i * 2 + j) * 4 + z

    def at(x, y, z, c):
        return (x, (y * 4 + z) * 2 + c)

    steps = []
    for a in range(3):
        for s in range(2):
            d = 1 if s == 0 else 3
            steps.append(((x + d) % 4 if a == 0 else x, (y + d) % 4 if a == 1 else y,
                          (z + d) % 4 if a == 2 else z))
    team = []
    for di, dj, dz in OFFSETS:
        i2, j2, z2 = (i + di) % 2, (j + dj) % 2, (z + dz) % 4
        team.append(((2 * i2 + (b0 + z2) % 2, 2 * j2 + (b1 + z2) % 2, z2),
                     (i2 * 2 + j2) * 4 + z2))
    partner = at(x, y, z, 1 - c)
    always = x < 4

    loads = [
        [pltpu.make_async_copy(h.at[n], ins.at[k, n], s_in.at[k, n])
         for k, h in enumerate((m_hbm, g1_hbm, g2_hbm))]
        for n in range(LAYERS)
    ]
    for group in loads:
        for copy in group:
            copy.start()
    barrier = pltpu.get_barrier_semaphore()
    greet = [partner]
    greet += [at(*p, c) for p in steps]
    greet += [at(*p, c) for p, _ in team]
    for who in greet:
        pl.semaphore_signal(barrier, inc=1, device_id=who, device_id_type=MESH)

    @pl.when(always)
    def _():
        for n in range(LAYERS):
            for copy in loads[n]:
                copy.wait()
            one = (momentum_decay * ins[0, n].astype(f32) + ins[1, n].astype(f32)).astype(bf16)
            y1_ref[n] = one
            y2_ref[n] = (momentum_decay * one.astype(f32) + ins[2, n].astype(f32)).astype(bf16)

    pl.semaphore_wait(barrier, len(greet))

    def send(src, dst, ss, rr, who):
        return pltpu.make_async_remote_copy(
            src_ref=src, dst_ref=dst, send_sem=ss, recv_sem=rr, device_id=who,
            device_id_type=MESH)

    row_copies = []
    for k, p in enumerate(steps):
        row_copies.append(send(
            y2_ref.at[lays[k // 2], pl.ds((k % 2) * 128, 128), :], rx.at[k],
            s_row.at[k], r_row.at[k], at(*p, c)))
    for copy in row_copies:
        copy.start()

    def heads(ns):
        grams = []
        norms = []
        for n in ns:
            v = y1_ref[n]
            g = lax.dot_general(v, v, (((1,), (1,)), ((), ())), preferred_element_type=f32)
            norm = jnp.sqrt(trace(g)) + norm_epsilon
            grams.append(g * (1.0 / (norm * norm)))
            norms.append(norm)
        for n, q, norm in zip(ns, polynomials(grams, mm), norms):
            high, low = split(q * (math.sqrt(max(ROWS, LATENT)) / norm))
            q1_ref[n, 0] = high
            q1_ref[n, 1] = low

    @pl.when(always)
    def _():
        for copy in row_copies:
            copy.wait()

    def gram_rows(i):
        total = None
        for v in [y2_ref.at[lay]] + [rx.at[k] for k in range(6)]:
            left = v[:, pl.ds(i * T, T)]
            right = v[:, pl.ds(i * T, LATENT - i * T)]
            g = lax.dot_general(left, right, (((0,), (0,)), ((), ())), preferred_element_type=f32)
            total = g if total is None else total + g
        return total

    @pl.when(always)
    def _():
        for i4 in range(4):
            g = gram_rows(i4)
            for j4 in range(i4, 4):
                b = BLOCKS.index((i4, j4))
                part[pl.ds(b * T, T), :] = g[:, (j4 - i4) * T:(j4 - i4 + 1) * T]

    theirs = pl.ds(pl.multiple_of((1 - c) * HALF, 8), HALF)
    mine = pl.ds(pl.multiple_of(c * HALF, 8), HALF)
    swap = send(part.at[theirs, :], core_in, s_core, r_core, partner)
    swap.start()
    swap.wait()
    own[...] = part[mine, :] + core_in[...]

    rs_copies = []
    for k, (p, t2) in enumerate(team):
        rs_copies.append(send(
            own.at[pl.ds(pl.multiple_of(t2 * PIECE, 8), PIECE), :], rs.at[k],
            s_rs.at[k], r_rs.at[k], at(*p, c)))
    for copy in rs_copies:
        copy.start()
    @pl.when(always)
    def _():
        heads((0, 1))

    for copy in rs_copies:
        copy.wait()
    total = own[pl.ds(pl.multiple_of(t * PIECE, 8), PIECE), :]
    for k in range(15):
        total = total + rs[k]
    here = pl.ds(pl.multiple_of(c * HALF + t * PIECE, 8), PIECE)
    gath[here, :] = total
    ag_copies = [
        send(gath.at[here, :], gath.at[here, :], s_ag.at[k], r_ag.at[k], at(*p, c))
        for k, (p, _) in enumerate(team)
    ]
    for copy in ag_copies:
        copy.start()
    @pl.when(always)
    def _():
        heads((2, 3))

    def relay(k, t3, core):
        there = pl.ds(pl.multiple_of(core * HALF + t3 * PIECE, 8), PIECE)
        return send(gath.at[there, :], gath.at[there, :], s_rel.at[k], r_rel.at[k], partner)

    relays = [(15, t)]
    for k, (di, dj, dz) in enumerate(OFFSETS):
        relays.append((k, (((i + di) % 2) * 2 + (j + dj) % 2) * 4 + (z + 4 - dz) % 4))
    for k, t3 in [relays[0]] + relays[:0:-1]:
        if k < 15:
            there = pl.ds(pl.multiple_of(c * HALF + t3 * PIECE, 8), PIECE)
            send(gath.at[there, :], gath.at[there, :], s_ag.at[k], r_ag.at[k],
                 at(*team[k][0], c)).wait_recv()
        relay(k, t3, c).start()
    for copy in ag_copies:
        copy.wait_send()
    for k, t3 in relays:
        relay(k, t3, c).wait_send()
    for k, t3 in relays:
        relay(k, t3, 1 - c).wait_recv()

    @pl.when(always)
    def _():
        gram = unpacked(gath[...])
        norm = jnp.sqrt(trace(gram)) + norm_epsilon
        q = polynomials([gram * (1.0 / (norm * norm))], mm_even)[0]
        parts = split(q * (math.sqrt(ALL_ROWS) / norm))
        for k in range(2):
            q2_ref[k] = parts[k]
            for b, (bi, bj) in enumerate(BLOCKS):
                packed[k, b * T:(b + 1) * T, :] = parts[k][
                    bi * T:(bi + 1) * T, bj * T:(bj + 1) * T]

    def part_of(a, s, h, core, src, ss, rr, who):
        rows = pl.ds(pl.multiple_of((s * 2 + core) * QUARTER + h * SHARE, 16), SHARE)
        return send(src.at[:, rows, :], rxq.at[a, :, rows, :], ss.at[a, s, h], rr.at[a, s, h], who)

    order = [(a, s, h) for h in range(SHARES) for a in range(3) for s in range(2)]
    q_copies = [
        part_of(a, s, h, c, packed, s_q, r_q, at(*steps[2 * a + s], c)) for a, s, h in order
    ]
    for copy in q_copies:
        copy.start()
    @pl.when(always)
    def _():
        w = y2_ref[lay]
        own2_ref[...] = dot(w, q2_ref[0]) + dot(w, q2_ref[1])
        for n in range(LAYERS):
            v = y1_ref[n]
            o1_ref[n] = dot(q1_ref[n, 0], v) + dot(q1_ref[n, 1], v)

    passed = []
    for copy, (a, s, h) in zip(q_copies, order):
        copy.wait()
        passed.append(part_of(a, s, h, c, rxq.at[a], s_qr, r_qr, partner))
        passed[-1].start()
    for copy in passed:
        copy.wait_send()
    for a, s, h in order:
        part_of(a, s, h, 1 - c, rxq.at[a], s_qr, r_qr, partner).wait_recv()


def finish(o1_ref, own2_ref, y2_ref, rxq, out1, out2, buf, sems):
    x = lax.axis_index("layer")
    head = lax.axis_index("head")
    y, z = head // 8, (head // 2) % 4
    b0, b1 = (x + z) % 2, (y + z) % 2
    copies = [pltpu.make_async_copy(
        own2_ref, out2.at[b0 + 2 * b1], sems.at[LAYERS])]
    for n in range(LAYERS):
        copies.append(pltpu.make_async_copy(o1_ref.at[n], out1.at[n], sems.at[n]))
    for copy in copies:
        copy.start()
    lays = [(1 - b0) + 2 * b1, b0 + 2 * (1 - b1), (1 - b0) + 2 * (1 - b1)]
    for a in range(3):
        w = y2_ref[lays[a]]
        buf[a] = dot(w, unpacked(rxq[a, 0])) + dot(w, unpacked(rxq[a, 1]))
        copies.append(pltpu.make_async_copy(buf.at[a], out2.at[lays[a]], sems.at[LAYERS + 1 + a]))
        copies[-1].start()
    for copy in copies:
        copy.wait()


def shards(momentum, grad_one, grad_two):
    vmem = pl.BlockSpec(memory_space=pltpu.VMEM)
    hbm = pl.BlockSpec(memory_space=pltpu.MemorySpace.HBM)
    dma = pltpu.SemaphoreType.DMA
    given = pl.pallas_call(
        exchange,
        out_shape=(
            jax.ShapeDtypeStruct((LAYERS, ROWS, LATENT), f32),
            jax.ShapeDtypeStruct((ROWS, LATENT), f32),
            jax.ShapeDtypeStruct((LAYERS, ROWS, LATENT), bf16),
            jax.ShapeDtypeStruct((3, 2, 2 * HALF, T), bf16),
        ),
        in_specs=[hbm] * 3,
        out_specs=(vmem,) * 4,
        scratch_shapes=[
            pltpu.VMEM((3, LAYERS, ROWS, LATENT), bf16),
            pltpu.VMEM((LAYERS, ROWS, LATENT), bf16),
            pltpu.VMEM((LAYERS, 2, ROWS, ROWS), bf16),
            pltpu.VMEM((6, 128, LATENT), bf16),
            pltpu.VMEM((2 * HALF, T), f32),
            pltpu.VMEM((HALF, T), f32),
            pltpu.VMEM((HALF, T), f32),
            pltpu.VMEM((15, PIECE, T), f32),
            pltpu.VMEM((2 * HALF, T), f32),
            pltpu.VMEM((2, 2 * HALF, T), bf16),
            pltpu.VMEM((2, LATENT, LATENT), bf16),
            dma((3, LAYERS)), dma((6,)), dma((6,)), dma, dma,
            dma((15,)), dma((15,)), dma((15,)), dma((15,)), dma((16,)), dma((16,)),
            dma((3, 2, SHARES)), dma((3, 2, SHARES)), dma((3, 2, SHARES)), dma((3, 2, SHARES)),
        ],
        compiler_params=pltpu.CompilerParams(
            collective_id=0, has_side_effects=True, vmem_limit_bytes=32 << 20),
        name="exchange",
    )(*[
        pltpu.with_memory_space_constraint(v, pltpu.MemorySpace.HBM)
        for v in (momentum, grad_one, grad_two)
    ])
    return pl.pallas_call(
        finish,
        out_shape=(jax.ShapeDtypeStruct((LAYERS, ROWS, LATENT), f32),) * 2,
        in_specs=[vmem] * 4,
        out_specs=(hbm,) * 2,
        scratch_shapes=[pltpu.VMEM((3, ROWS, LATENT), f32), dma((LAYERS + 4,))],
        compiler_params=pltpu.CompilerParams(vmem_limit_bytes=12 << 20),
        name="finish",
    )(*given)


def solution(mesh):
    spec = P(None, ("layer", "head"), None)
    return jax.shard_map(
        shards, mesh=mesh, in_specs=(spec,) * 3, out_specs=(spec,) * 2, check_vma=False
    )
```

```python
import functools
import math

import jax
import jax.numpy as jnp
from jax import lax
from jax.experimental import pallas as pl
from jax.experimental.pallas import tpu as pltpu
from jax.sharding import PartitionSpec as P

NS_ITERS = 5
quintic_a = 3.4445
quintic_b = -4.775
quintic_c = 2.0315
norm_epsilon = 1e-07
momentum_decay = 0.95

bf16 = jnp.bfloat16
f32 = jnp.float32
MESH = pl.DeviceIdType.MESH
LAYERS, ROWS, LATENT = 4, 256, 512
ALL_ROWS = 32768
T = 128
BLOCKS = [(i, j) for i in range(4) for j in range(i, 4)]
SENT = [(0, 0), (0, 1), (1, 1), (0, 2), (0, 3), (2, 2), (2, 3), (3, 3), (2, 1), (3, 1)]
HALF = len(BLOCKS) * T // 2
PIECE = HALF // 16
QUARTER = HALF // 2
SHARES = 4
CHUNK = 64
SHARE = QUARTER // SHARES
OFFSETS = [(1, 1, 2), (1, 1, 0), (1, 0, 2), (0, 1, 2)]
OFFSETS += [(i, j, z) for z in (1, 3) for i in (0, 1) for j in (0, 1)]
OFFSETS += [(1, 0, 0), (0, 1, 0), (0, 0, 2)]


def split(x):
    high = x.astype(bf16)
    return high, (x - high.astype(f32)).astype(bf16)


def dot(x, y):
    return jnp.dot(x, y, preferred_element_type=f32)


def dot3(x, y):
    return dot(x[0], y[0]) + (dot(x[0], y[1]) + dot(x[1], y[0]))


def mm(x, y):
    return dot3(x, y)


def mm_even(x, y):
    h = x[0].shape[0] // 2
    top = dot3([t[:h] for t in x], y)
    low = dot3([t[h:] for t in x], [t[:, h:] for t in y])
    return jnp.concatenate([top, jnp.concatenate([top[:, h:].T, low], 1)], 0)


def square(x):
    high, low = x
    cross = dot(high, low)
    return dot(high, high) + (cross + cross.T)


def square_even(x):
    high, low = x
    h = high.shape[0] // 2
    cross = dot(high, low)
    top, last = dot(high[:h], high), dot(high[h:], high[:, h:])
    first = top[:, :h] + (cross[:h, :h] + cross[:h, :h].T)
    side = top[:, h:] + (cross[:h, h:] + cross[h:, :h].T)
    last = last + (cross[h:, h:] + cross[h:, h:].T)
    return jnp.concatenate(
        [jnp.concatenate([first, side], 1), jnp.concatenate([side.T, last], 1)], 0)


def eye(n):
    rows = lax.broadcasted_iota(jnp.int32, (n, n), 0)
    return rows == lax.broadcasted_iota(jnp.int32, (n, n), 1)


def half_polynomial(gram, product, scratch, start):
    n = gram.shape[0]
    diag = jnp.where(eye(n), f32(quintic_a), f32(0.0))
    s, q = gram, None
    for k in range(NS_ITERS):
        part = split(s)
        m = diag + (quintic_b * s + quintic_c * square_even(part))
        if k == 0:
            scratch[...] = m
        ms = split(m)
        if k < NS_ITERS - 1:
            s = product(split(product(part, ms)), ms)
        q = scratch[pl.ds(start, n // 2), :] if k == 0 else dot3(split(q), ms)
    return q


def polynomials(grams, product):
    n = grams[0].shape[0]
    diag = jnp.where(eye(n), f32(quintic_a), f32(0.0))
    s, q = list(grams), [None] * len(grams)
    for k in range(NS_ITERS):
        parts = [split(t) for t in s]
        m = [
            diag + (quintic_b * t + quintic_c * square(u)) for t, u in zip(s, parts)
        ]
        ms = [split(t) for t in m]
        if k < NS_ITERS - 1:
            r = [split(product(u, v)) for u, v in zip(parts, ms)]
            s = [product(u, v) for u, v in zip(r, ms)]
        q = m if k == 0 else [product(split(u), v) for u, v in zip(q, ms)]
    return q


def unpacked(blocks, order=BLOCKS):
    tiles = {}
    for b, (i, j) in enumerate(order):
        v = blocks[b * T:(b + 1) * T, :]
        tiles[i, j] = v
        if i != j:
            tiles[j, i] = v.T
    return jnp.concatenate(
        [jnp.concatenate([tiles[i, j] for j in range(4)], 1) for i in range(4)], 0)


def restored(blocks):
    return unpacked(blocks, SENT)


def trace(x):
    return jnp.sum(jnp.where(eye(x.shape[0]), x, f32(0.0)))


def exchange(
    m_hbm, g1_hbm, g2_hbm, o1_ref, own2_ref, y2_ref, rxq,
    ins, y1_ref, q1_ref, rx, part, core_in, own, rs, gath, q_full, q_half, rounds,
    s_in, s_row, r_row, s_core, r_core, s_rs, r_rs, s_ag, r_ag, s_rel, r_rel,
    s_q, r_q, s_qr, r_qr, s_own, r_own,
):
    x = lax.axis_index("layer")
    head = lax.axis_index("head")
    y, z, c = head // 8, (head // 2) % 4, head % 2
    b0, b1 = (x + z) % 2, (y + z) % 2
    lay = b0 + 2 * b1
    lays = [(1 - b0) + 2 * b1, b0 + 2 * (1 - b1), (1 - b0) + 2 * (1 - b1)]
    i, j = x // 2, y // 2
    t = (i * 2 + j) * 4 + z

    def at(x, y, z, c):
        return (x, (y * 4 + z) * 2 + c)

    steps = []
    for a in range(3):
        for s in range(2):
            d = 1 if s == 0 else 3
            steps.append(((x + d) % 4 if a == 0 else x, (y + d) % 4 if a == 1 else y,
                          (z + d) % 4 if a == 2 else z))
    team = []
    for di, dj, dz in OFFSETS:
        i2, j2, z2 = (i + di) % 2, (j + dj) % 2, (z + dz) % 4
        team.append(((2 * i2 + (b0 + z2) % 2, 2 * j2 + (b1 + z2) % 2, z2),
                     (i2 * 2 + j2) * 4 + z2))
    partner = at(x, y, z, 1 - c)
    always = x < 4

    def phase(name):
        def run(body):
            with jax.named_scope(name):
                pl.when(always)(body)
        return run


    barrier = pltpu.get_barrier_semaphore()
    greet = [partner]
    greet += [at(*p, c) for p in steps]
    for who in greet:
        pl.semaphore_signal(barrier, inc=1, device_id=who, device_id_type=MESH)

    turn = lays + [lay]
    loads = [
        [pltpu.make_async_copy(h.at[n], ins.at[k, w], s_in.at[k, w])
         for k, h in enumerate((m_hbm, g1_hbm, g2_hbm))]
        for w, n in enumerate(turn)
    ]
    for group in loads:
        for copy in group:
            copy.start()
    def send(src, dst, ss, rr, who):
        return pltpu.make_async_remote_copy(
            src_ref=src, dst_ref=dst, send_sem=ss, recv_sem=rr, device_id=who,
            device_id_type=MESH)

    row_copies = [
        [send(y2_ref.at[lays[k // 2], pl.ds((k % 2) * 128 + h * CHUNK, CHUNK), :],
              rx.at[h, pl.ds(k * CHUNK, CHUNK), :], s_row.at[h, k], r_row.at[h, k], at(*p, c))
         for k, p in enumerate(steps)]
        for h in range(2)
    ]

    near = [at(*p, c) for p in steps]
    far = [at((x + 2) % 4, y, z, c), at(x, (y + 2) % 4, z, c), at(x, y, (z + 2) % 4, c)]
    told = [near, near + far, far[:1]]

    def tell(k):
        for who in told[k]:
            pl.semaphore_signal(rounds.at[k], inc=1, device_id=who, device_id_type=MESH)

    @phase("w_barrier")
    def _():
        pl.semaphore_wait(barrier, len(greet))
        tell(0)

    for w, n in enumerate(turn):
        @phase("p01")
        def _(w=w, n=n):
            for copy in loads[w]:
                copy.wait()
            one = (momentum_decay * ins[0, w].astype(f32) + ins[1, w].astype(f32)).astype(bf16)
            y1_ref[n] = one
            y2_ref[n] = (momentum_decay * one.astype(f32) + ins[2, w].astype(f32)).astype(bf16)

        if w == 0:
            @phase("w_tell")
            def _():
                pl.semaphore_wait(rounds.at[0], len(told[0]))
                tell(1)
        if w < 3:
            for h in range(2):
                for k in (2 * w, 2 * w + 1):
                    row_copies[h][k].start()

    @phase("w_rounds")
    def _():
        pl.semaphore_wait(rounds.at[1], len(told[1]))
        tell(2)

    def heads(ns):
        grams = []
        norms = []
        for n in ns:
            v = y1_ref[n]
            g = lax.dot_general(v, v, (((1,), (1,)), ((), ())), preferred_element_type=f32)
            norm = jnp.sqrt(trace(g)) + norm_epsilon
            grams.append(g * (1.0 / (norm * norm)))
            norms.append(norm)
        for n, q, norm in zip(ns, polynomials(grams, mm), norms):
            high, low = split(q * (math.sqrt(max(ROWS, LATENT)) / norm))
            q1_ref[n, 0] = high
            q1_ref[n, 1] = low

    def gram_of(views, first):
        for i4 in range(4):
            total = None
            for v in views:
                g = lax.dot_general(
                    v[:, pl.ds(i4 * T, T)], v[:, pl.ds(i4 * T, LATENT - i4 * T)],
                    (((0,), (0,)), ((), ())), preferred_element_type=f32)
                total = g if total is None else total + g
            for j4 in range(i4, 4):
                rows = pl.ds(BLOCKS.index((i4, j4)) * T, T)
                value = total[:, (j4 - i4) * T:(j4 - i4 + 1) * T]
                part[rows, :] = value if first else part[rows, :] + value

    @phase("w_rows0")
    def _():
        for copy in row_copies[0]:
            copy.wait()

    @phase("p02")
    def _():
        gram_of([y2_ref.at[lay], rx.at[0]], True)

    @phase("w_rows1")
    def _():
        for copy in row_copies[1]:
            copy.wait()

    @phase("p03")
    def _():
        gram_of([rx.at[1]], False)

    theirs = pl.ds(pl.multiple_of((1 - c) * HALF, 8), HALF)
    mine = pl.ds(pl.multiple_of(c * HALF, 8), HALF)
    swap = send(part.at[theirs, :], core_in, s_core, r_core, partner)
    swap.start()
    @phase("w_swap")
    def _():
        swap.wait()
        own[...] = part[mine, :] + core_in[...]

    rs_copies = []
    for k, (p, t2) in enumerate(team):
        rs_copies.append(send(
            own.at[pl.ds(pl.multiple_of(t2 * PIECE, 8), PIECE), :], rs.at[k],
            s_rs.at[k], r_rs.at[k], at(*p, c)))
    pl.semaphore_wait(rounds.at[2], len(told[2]))
    for copy in rs_copies:
        copy.start()
    @phase("p04")
    def _():
        heads((0, 1))

    @phase("w_rs")
    def _():
        for copy in rs_copies:
            copy.wait()

    total = own[pl.ds(pl.multiple_of(t * PIECE, 8), PIECE), :]
    for k in range(15):
        total = total + rs[k]
    here = pl.ds(pl.multiple_of(c * HALF + t * PIECE, 8), PIECE)
    gath[here, :] = total
    ag_copies = [
        send(gath.at[here, :], gath.at[here, :], s_ag.at[k], r_ag.at[k], at(*p, c))
        for k, (p, _) in enumerate(team)
    ]
    for copy in ag_copies:
        copy.start()
    @phase("p05")
    def _():
        heads((2, 3))

    def relay(k, t3, core):
        there = pl.ds(pl.multiple_of(core * HALF + t3 * PIECE, 8), PIECE)
        return send(gath.at[there, :], gath.at[there, :], s_rel.at[k], r_rel.at[k], partner)

    relays = [(15, t)]
    for k, (di, dj, dz) in enumerate(OFFSETS):
        relays.append((k, (((i + di) % 2) * 2 + (j + dj) % 2) * 4 + (z + 4 - dz) % 4))
    @phase("w_ag")
    def _():
        for k, t3 in [relays[0]] + relays[:0:-1]:
            if k < 15:
                there = pl.ds(pl.multiple_of(c * HALF + t3 * PIECE, 8), PIECE)
                send(gath.at[there, :], gath.at[there, :], s_ag.at[k], r_ag.at[k],
                     at(*team[k][0], c)).wait_recv()
            relay(k, t3, c).start()

    @phase("w_relay")
    def _():
        for copy in ag_copies:
            copy.wait_send()
        for k, t3 in relays:
            relay(k, t3, c).wait_send()
        for k, t3 in relays:
            relay(k, t3, 1 - c).wait_recv()

    @phase("p06")
    def _():
        gram = unpacked(gath[...])
        norm = jnp.sqrt(trace(gram)) + norm_epsilon
        q = half_polynomial(
            gram * (1.0 / (norm * norm)), mm_even, q_full, pl.multiple_of(c * 256, 256))
        parts = split(q * (math.sqrt(ALL_ROWS) / norm))
        for k in range(2):
            q_half[k] = parts[k]
            where = [(0, 256 * c), (0, 256 * c + T), (T, 256 * c + T), (0, 256 - T * c),
                     (T * c, 384 - 256 * c)]
            for b, (row, column) in enumerate(where):
                tile = q_half[k, pl.ds(pl.multiple_of(row, T), T),
                              pl.ds(pl.multiple_of(column, T), T)]
                rxq[3, k, pl.ds(pl.multiple_of(c * HALF + b * T, T), T), :] = tile

    def part_of(a, s, h, core, src, ss, rr, who):
        rows = pl.ds(pl.multiple_of(core * HALF + s * QUARTER + h * SHARE, 16), SHARE)
        return send(rxq.at[src, :, rows, :], rxq.at[a, :, rows, :], ss.at[a, s, h],
                    rr.at[a, s, h], who)

    order = [(a, s, h) for h in range(SHARES) for a in range(3) for s in range(2)]
    q_copies = [part_of(a, s, h, c, 3, s_q, r_q, at(*steps[2 * a + s], c)) for a, s, h in order]
    for copy in q_copies:
        copy.start()
    own_half = [send(rxq.at[3, :, rows, :], rxq.at[3, :, rows, :], s_own, r_own, partner)
                for rows in (mine, theirs)]
    own_half[0].start()

    @phase("p07")
    def _():
        for n in range(LAYERS):
            v = y1_ref[n]
            o1_ref[n] = dot(q1_ref[n, 0], v) + dot(q1_ref[n, 1], v)

    @phase("w_ownhalf")
    def _():
        own_half[0].wait_send()
        own_half[1].wait_recv()

    @phase("p08")
    def _():
        w = y2_ref[lay]
        own2_ref[...] = dot(w, restored(rxq[3, 0])) + dot(w, restored(rxq[3, 1]))

    passed = [part_of(a, s, h, c, a, s_qr, r_qr, partner) for a, s, h in order]

    @phase("w_q")
    def _():
        for copy, onward in zip(q_copies, passed):
            copy.wait()
            onward.start()

    @phase("w_final")
    def _():
        for copy in passed:
            copy.wait_send()
        for a, s, h in order:
            part_of(a, s, h, 1 - c, a, s_qr, r_qr, partner).wait_recv()

def finish(o1_ref, own2_ref, y2_ref, rxq, out1, out2, buf, sems):
    x = lax.axis_index("layer")
    head = lax.axis_index("head")
    y, z = head // 8, (head // 2) % 4
    b0, b1 = (x + z) % 2, (y + z) % 2
    copies = [pltpu.make_async_copy(
        own2_ref, out2.at[b0 + 2 * b1], sems.at[LAYERS])]
    for n in range(LAYERS):
        copies.append(pltpu.make_async_copy(o1_ref.at[n], out1.at[n], sems.at[n]))
    for copy in copies:
        copy.start()
    lays = [(1 - b0) + 2 * b1, b0 + 2 * (1 - b1), (1 - b0) + 2 * (1 - b1)]
    for a in range(3):
        w = y2_ref[lays[a]]
        buf[a] = dot(w, restored(rxq[a, 0])) + dot(w, restored(rxq[a, 1]))
        copies.append(pltpu.make_async_copy(buf.at[a], out2.at[lays[a]], sems.at[LAYERS + 1 + a]))
        copies[-1].start()
    for copy in copies:
        copy.wait()


def shards(momentum, grad_one, grad_two):
    vmem = pl.BlockSpec(memory_space=pltpu.VMEM)
    hbm = pl.BlockSpec(memory_space=pltpu.MemorySpace.HBM)
    dma = pltpu.SemaphoreType.DMA
    given = pl.pallas_call(
        exchange,
        out_shape=(
            jax.ShapeDtypeStruct((LAYERS, ROWS, LATENT), f32),
            jax.ShapeDtypeStruct((ROWS, LATENT), f32),
            jax.ShapeDtypeStruct((LAYERS, ROWS, LATENT), bf16),
            jax.ShapeDtypeStruct((4, 2, 2 * HALF, T), bf16),
        ),
        in_specs=[hbm] * 3,
        out_specs=(vmem,) * 4,
        scratch_shapes=[
            pltpu.VMEM((3, LAYERS, ROWS, LATENT), bf16),
            pltpu.VMEM((LAYERS, ROWS, LATENT), bf16),
            pltpu.VMEM((LAYERS, 2, ROWS, ROWS), bf16),
            pltpu.VMEM((2, 6 * CHUNK, LATENT), bf16),
            pltpu.VMEM((2 * HALF, T), f32),
            pltpu.VMEM((HALF, T), f32),
            pltpu.VMEM((HALF, T), f32),
            pltpu.VMEM((15, PIECE, T), f32),
            pltpu.VMEM((2 * HALF, T), f32),
            pltpu.VMEM((LATENT, LATENT), f32),
            pltpu.VMEM((2, LATENT // 2, LATENT), bf16),
            pltpu.SemaphoreType.REGULAR((3,)),
            dma((3, LAYERS)), dma((2, 6)), dma((2, 6)), dma, dma,
            dma((15,)), dma((15,)), dma((15,)), dma((15,)), dma((16,)), dma((16,)),
            dma((3, 2, SHARES)), dma((3, 2, SHARES)), dma((3, 2, SHARES)), dma((3, 2, SHARES)),
            dma, dma,
        ],
        compiler_params=pltpu.CompilerParams(
            collective_id=0, has_side_effects=True, vmem_limit_bytes=32 << 20),
        name="exchange",
    )(*[
        pltpu.with_memory_space_constraint(v, pltpu.MemorySpace.HBM)
        for v in (momentum, grad_one, grad_two)
    ])
    return pl.pallas_call(
        finish,
        out_shape=(jax.ShapeDtypeStruct((LAYERS, ROWS, LATENT), f32),) * 2,
        in_specs=[vmem] * 4,
        out_specs=(hbm,) * 2,
        scratch_shapes=[pltpu.VMEM((3, ROWS, LATENT), f32), dma((LAYERS + 4,))],
        compiler_params=pltpu.CompilerParams(vmem_limit_bytes=12 << 20),
        name="finish",
    )(*given)


def solution(mesh):
    spec = P(None, ("layer", "head"), None)
    return jax.shard_map(
        shards, mesh=mesh, in_specs=(spec,) * 3, out_specs=(spec,) * 2, check_vma=False
    )
```

```python
import functools
import math

import jax
import jax.numpy as jnp
from jax import lax
from jax.experimental import pallas as pl
from jax.experimental.pallas import tpu as pltpu
from jax.sharding import PartitionSpec as P

NS_ITERS = 5
quintic_a = 3.4445
quintic_b = -4.775
quintic_c = 2.0315
norm_epsilon = 1e-07
momentum_decay = 0.95

bf16 = jnp.bfloat16
f32 = jnp.float32
MESH = pl.DeviceIdType.MESH
LAYERS, ROWS, LATENT = 4, 256, 512
ALL_ROWS = 32768
T = 128
BLOCKS = [(i, j) for i in range(4) for j in range(i, 4)]
HALF = len(BLOCKS) * T // 2
PIECE = HALF // 16
CHUNK = 64
OFFSETS = [(1, 1, 2), (1, 1, 0), (1, 0, 2), (0, 1, 2)]
OFFSETS += [(i, j, z) for z in (1, 3) for i in (0, 1) for j in (0, 1)]
OFFSETS += [(1, 0, 0), (0, 1, 0), (0, 0, 2)]


def split(x):
    high = x.astype(bf16)
    return high, (x - high.astype(f32)).astype(bf16)


def dot(x, y):
    return jnp.dot(x, y, preferred_element_type=f32)


def dot3(x, y):
    return dot(x[0], y[0]) + (dot(x[0], y[1]) + dot(x[1], y[0]))


def mm(x, y):
    return dot3(x, y)


def mm_even(x, y):
    h = x[0].shape[0] // 2
    top = dot3([t[:h] for t in x], y)
    low = dot3([t[h:] for t in x], [t[:, h:] for t in y])
    return jnp.concatenate([top, jnp.concatenate([top[:, h:].T, low], 1)], 0)


def square_even(x):
    high, low = x
    h = high.shape[0] // 2
    cross = dot(high, low)
    top, last = dot(high[:h], high), dot(high[h:], high[:, h:])
    first = top[:, :h] + (cross[:h, :h] + cross[:h, :h].T)
    side = top[:, h:] + (cross[:h, h:] + cross[h:, :h].T)
    last = last + (cross[h:, h:] + cross[h:, h:].T)
    return jnp.concatenate(
        [jnp.concatenate([first, side], 1), jnp.concatenate([side.T, last], 1)], 0)


def eye(n):
    rows = lax.broadcasted_iota(jnp.int32, (n, n), 0)
    return rows == lax.broadcasted_iota(jnp.int32, (n, n), 1)


def layer_polynomial(gram):
    diag = jnp.where(eye(gram.shape[0]), f32(quintic_a), f32(0.0))
    s, q = gram, None
    for k in range(NS_ITERS):
        part = split(s)
        m = diag + (quintic_b * s + quintic_c * square_even(part))
        ms = split(m)
        if k < NS_ITERS - 1:
            s = mm_even(split(mm_even(part, ms)), ms)
        q = m if k == 0 else mm_even(split(q), ms)
    return q


def polynomials(grams, product):
    n = grams[0].shape[0]
    diag = jnp.where(eye(n), f32(quintic_a), f32(0.0))
    s, q = list(grams), [None] * len(grams)
    for k in range(NS_ITERS):
        parts = [split(t) for t in s]
        m = [
            diag + (quintic_b * t + quintic_c * product(u, u)) for t, u in zip(s, parts)
        ]
        ms = [split(t) for t in m]
        if k < NS_ITERS - 1:
            r = [split(product(u, v)) for u, v in zip(parts, ms)]
            s = [product(u, v) for u, v in zip(r, ms)]
        q = m if k == 0 else [product(split(u), v) for u, v in zip(q, ms)]
    return q


def unpacked(blocks):
    tiles = {}
    for b, (i, j) in enumerate(BLOCKS):
        v = blocks[b * T:(b + 1) * T, :]
        tiles[i, j] = v
        if i != j:
            tiles[j, i] = v.T
    return jnp.concatenate(
        [jnp.concatenate([tiles[i, j] for j in range(4)], 1) for i in range(4)], 0)


def trace(x):
    return jnp.sum(jnp.where(eye(x.shape[0]), x, f32(0.0)))


def exchange(
    m_hbm, g1_hbm, g2_hbm, o1_ref, own2_ref, got,
    ins, y1_ref, y2_ref, q1_ref, rx, tx, part, core_in, own, rs, gath, q2_ref, rounds,
    s_in, s_row, r_row, s_core, r_core, s_rs, r_rs, s_ag, r_ag, s_rel, r_rel,
    s_q, r_q,
):
    x = lax.axis_index("layer")
    head = lax.axis_index("head")
    y, z, c = head // 8, (head // 2) % 4, head % 2
    b0, b1 = (x + z) % 2, (y + z) % 2
    lay = b0 + 2 * b1
    lays = [(1 - b0) + 2 * b1, b0 + 2 * (1 - b1), (1 - b0) + 2 * (1 - b1)]
    i, j = x // 2, y // 2
    t = (i * 2 + j) * 4 + z

    def at(x, y, z, c):
        return (x, (y * 4 + z) * 2 + c)

    steps = []
    for a in range(3):
        for s in range(2):
            d = 1 if s == 0 else 3
            steps.append(((x + d) % 4 if a == 0 else x, (y + d) % 4 if a == 1 else y,
                          (z + d) % 4 if a == 2 else z))
    team = []
    for di, dj, dz in OFFSETS:
        i2, j2, z2 = (i + di) % 2, (j + dj) % 2, (z + dz) % 4
        team.append(((2 * i2 + (b0 + z2) % 2, 2 * j2 + (b1 + z2) % 2, z2),
                     (i2 * 2 + j2) * 4 + z2))
    partner = at(x, y, z, 1 - c)
    always = x < 4

    def phase(name):
        def run(body):
            with jax.named_scope(name):
                pl.when(always)(body)
        return run


    barrier = pltpu.get_barrier_semaphore()
    greet = [partner]
    greet += [at(*p, c) for p in steps]
    for who in greet:
        pl.semaphore_signal(barrier, inc=1, device_id=who, device_id_type=MESH)

    turn = lays + [lay]
    loads = [
        [pltpu.make_async_copy(h.at[n], ins.at[k, w], s_in.at[k, w])
         for k, h in enumerate((m_hbm, g1_hbm, g2_hbm))]
        for w, n in enumerate(turn)
    ]
    for group in loads:
        for copy in group:
            copy.start()
    def send(src, dst, ss, rr, who):
        return pltpu.make_async_remote_copy(
            src_ref=src, dst_ref=dst, send_sem=ss, recv_sem=rr, device_id=who,
            device_id_type=MESH)

    row_copies = [
        [send(y2_ref.at[lays[k // 2], pl.ds((k % 2) * 128 + h * CHUNK, CHUNK), :],
              rx.at[h, pl.ds(k * CHUNK, CHUNK), :], s_row.at[h, k], r_row.at[h, k], at(*p, c))
         for k, p in enumerate(steps)]
        for h in range(2)
    ]

    near = [at(*p, c) for p in steps]
    far = [at((x + 2) % 4, y, z, c), at(x, (y + 2) % 4, z, c), at(x, y, (z + 2) % 4, c)]
    told = [near, near + far, far[:1]]

    def tell(k):
        for who in told[k]:
            pl.semaphore_signal(rounds.at[k], inc=1, device_id=who, device_id_type=MESH)

    @phase("w_barrier")
    def _():
        pl.semaphore_wait(barrier, len(greet))
        tell(0)

    for w, n in enumerate(turn):
        @phase("p01")
        def _(w=w, n=n):
            for copy in loads[w]:
                copy.wait()
            one = (momentum_decay * ins[0, w].astype(f32) + ins[1, w].astype(f32)).astype(bf16)
            y1_ref[n] = one
            y2_ref[n] = (momentum_decay * one.astype(f32) + ins[2, w].astype(f32)).astype(bf16)

        if w == 0:
            @phase("w_tell")
            def _():
                pl.semaphore_wait(rounds.at[0], len(told[0]))
                tell(1)
        if w < 3:
            for h in range(2):
                for k in (2 * w, 2 * w + 1):
                    row_copies[h][k].start()

    @phase("w_rounds")
    def _():
        pl.semaphore_wait(rounds.at[1], len(told[1]))
        tell(2)

    def heads(ns):
        grams = []
        norms = []
        for n in ns:
            v = y1_ref[n]
            g = lax.dot_general(v, v, (((1,), (1,)), ((), ())), preferred_element_type=f32)
            norm = jnp.sqrt(trace(g)) + norm_epsilon
            grams.append(g * (1.0 / (norm * norm)))
            norms.append(norm)
        for n, q, norm in zip(ns, polynomials(grams, mm), norms):
            high, low = split(q * (math.sqrt(max(ROWS, LATENT)) / norm))
            q1_ref[n, 0] = high
            q1_ref[n, 1] = low

    def gram_of(views, first):
        for i4 in range(4):
            total = None
            for v in views:
                g = lax.dot_general(
                    v[:, pl.ds(i4 * T, T)], v[:, pl.ds(i4 * T, LATENT - i4 * T)],
                    (((0,), (0,)), ((), ())), preferred_element_type=f32)
                total = g if total is None else total + g
            for j4 in range(i4, 4):
                rows = pl.ds(BLOCKS.index((i4, j4)) * T, T)
                value = total[:, (j4 - i4) * T:(j4 - i4 + 1) * T]
                part[rows, :] = value if first else part[rows, :] + value

    @phase("w_rows0")
    def _():
        for copy in row_copies[0]:
            copy.wait()

    @phase("p02")
    def _():
        gram_of([y2_ref.at[lay], rx.at[0]], True)

    @phase("w_rows1")
    def _():
        for copy in row_copies[1]:
            copy.wait()

    @phase("p03")
    def _():
        gram_of([rx.at[1]], False)

    theirs = pl.ds(pl.multiple_of((1 - c) * HALF, 8), HALF)
    mine = pl.ds(pl.multiple_of(c * HALF, 8), HALF)
    swap = send(part.at[theirs, :], core_in, s_core, r_core, partner)
    swap.start()
    @phase("w_swap")
    def _():
        swap.wait()
        own[...] = part[mine, :] + core_in[...]

    rs_copies = []
    for k, (p, t2) in enumerate(team):
        rs_copies.append(send(
            own.at[pl.ds(pl.multiple_of(t2 * PIECE, 8), PIECE), :], rs.at[k],
            s_rs.at[k], r_rs.at[k], at(*p, c)))
    pl.semaphore_wait(rounds.at[2], len(told[2]))
    for copy in rs_copies:
        copy.start()
    @phase("p04")
    def _():
        heads((0, 1))

    @phase("w_rs")
    def _():
        for copy in rs_copies:
            copy.wait()

    total = own[pl.ds(pl.multiple_of(t * PIECE, 8), PIECE), :]
    for k in range(15):
        total = total + rs[k]
    here = pl.ds(pl.multiple_of(c * HALF + t * PIECE, 8), PIECE)
    gath[here, :] = total
    ag_copies = [
        send(gath.at[here, :], gath.at[here, :], s_ag.at[k], r_ag.at[k], at(*p, c))
        for k, (p, _) in enumerate(team)
    ]
    for copy in ag_copies:
        copy.start()
    @phase("p05")
    def _():
        heads((2, 3))

    def relay(k, t3, core):
        there = pl.ds(pl.multiple_of(core * HALF + t3 * PIECE, 8), PIECE)
        return send(gath.at[there, :], gath.at[there, :], s_rel.at[k], r_rel.at[k], partner)

    relays = [(15, t)]
    for k, (di, dj, dz) in enumerate(OFFSETS):
        relays.append((k, (((i + di) % 2) * 2 + (j + dj) % 2) * 4 + (z + 4 - dz) % 4))
    @phase("w_ag")
    def _():
        for k, t3 in [relays[0]] + relays[:0:-1]:
            if k < 15:
                there = pl.ds(pl.multiple_of(c * HALF + t3 * PIECE, 8), PIECE)
                send(gath.at[there, :], gath.at[there, :], s_ag.at[k], r_ag.at[k],
                     at(*team[k][0], c)).wait_recv()
            relay(k, t3, c).start()

    @phase("w_relay")
    def _():
        for copy in ag_copies:
            copy.wait_send()
        for k, t3 in relays:
            relay(k, t3, c).wait_send()
        for k, t3 in relays:
            relay(k, t3, 1 - c).wait_recv()

    @phase("p06")
    def _():
        gram = unpacked(gath[...])
        norm = jnp.sqrt(trace(gram)) + norm_epsilon
        q = layer_polynomial(gram * (1.0 / (norm * norm)))
        q2_ref[0], q2_ref[1] = split(q * (math.sqrt(ALL_ROWS) / norm))

    back = []
    for h in range(2):
        @phase("p07")
        def _(h=h):
            w = rx[h]
            tx[h] = (dot(w, q2_ref[0]) + dot(w, q2_ref[1])).astype(bf16)

        for k, p in enumerate(steps):
            back.append(send(
                tx.at[h, pl.ds(k * CHUNK, CHUNK), :],
                got.at[k // 2, pl.ds((k % 2) * 128 + h * CHUNK, CHUNK), :],
                s_q.at[h, k], r_q.at[h, k], at(*steps[k ^ 1], c)))
            back[-1].start()

    @phase("p08")
    def _():
        w = y2_ref[lay]
        own2_ref[...] = dot(w, q2_ref[0]) + dot(w, q2_ref[1])
        for n in range(LAYERS):
            v = y1_ref[n]
            o1_ref[n] = dot(q1_ref[n, 0], v) + dot(q1_ref[n, 1], v)

    @phase("w_back")
    def _():
        for copy in back:
            copy.wait()


def finish(o1_ref, own2_ref, got, out1, out2, buf, sems):
    x = lax.axis_index("layer")
    head = lax.axis_index("head")
    y, z = head // 8, (head // 2) % 4
    b0, b1 = (x + z) % 2, (y + z) % 2
    copies = [pltpu.make_async_copy(
        own2_ref, out2.at[b0 + 2 * b1], sems.at[LAYERS])]
    for n in range(LAYERS):
        copies.append(pltpu.make_async_copy(o1_ref.at[n], out1.at[n], sems.at[n]))
    for copy in copies:
        copy.start()
    lays = [(1 - b0) + 2 * b1, b0 + 2 * (1 - b1), (1 - b0) + 2 * (1 - b1)]
    for a in range(3):
        buf[a] = got[a].astype(f32)
        copies.append(pltpu.make_async_copy(buf.at[a], out2.at[lays[a]], sems.at[LAYERS + 1 + a]))
        copies[-1].start()
    for copy in copies:
        copy.wait()


def shards(momentum, grad_one, grad_two):
    vmem = pl.BlockSpec(memory_space=pltpu.VMEM)
    hbm = pl.BlockSpec(memory_space=pltpu.MemorySpace.HBM)
    dma = pltpu.SemaphoreType.DMA
    given = pl.pallas_call(
        exchange,
        out_shape=(
            jax.ShapeDtypeStruct((LAYERS, ROWS, LATENT), f32),
            jax.ShapeDtypeStruct((ROWS, LATENT), f32),
            jax.ShapeDtypeStruct((3, ROWS, LATENT), bf16),
        ),
        in_specs=[hbm] * 3,
        out_specs=(vmem,) * 3,
        scratch_shapes=[
            pltpu.VMEM((3, LAYERS, ROWS, LATENT), bf16),
            pltpu.VMEM((LAYERS, ROWS, LATENT), bf16),
            pltpu.VMEM((LAYERS, ROWS, LATENT), bf16),
            pltpu.VMEM((LAYERS, 2, ROWS, ROWS), bf16),
            pltpu.VMEM((2, 6 * CHUNK, LATENT), bf16),
            pltpu.VMEM((2, 6 * CHUNK, LATENT), bf16),
            pltpu.VMEM((2 * HALF, T), f32),
            pltpu.VMEM((HALF, T), f32),
            pltpu.VMEM((HALF, T), f32),
            pltpu.VMEM((15, PIECE, T), f32),
            pltpu.VMEM((2 * HALF, T), f32),
            pltpu.VMEM((2, LATENT, LATENT), bf16),
            pltpu.SemaphoreType.REGULAR((3,)),
            dma((3, LAYERS)), dma((2, 6)), dma((2, 6)), dma, dma,
            dma((15,)), dma((15,)), dma((15,)), dma((15,)), dma((16,)), dma((16,)),
            dma((2, 6)), dma((2, 6)),
        ],
        compiler_params=pltpu.CompilerParams(
            collective_id=0, has_side_effects=True, vmem_limit_bytes=32 << 20),
        name="exchange",
    )(*[
        pltpu.with_memory_space_constraint(v, pltpu.MemorySpace.HBM)
        for v in (momentum, grad_one, grad_two)
    ])
    return pl.pallas_call(
        finish,
        out_shape=(jax.ShapeDtypeStruct((LAYERS, ROWS, LATENT), f32),) * 2,
        in_specs=[vmem] * 3,
        out_specs=(hbm,) * 2,
        scratch_shapes=[pltpu.VMEM((3, ROWS, LATENT), f32), dma((LAYERS + 4,))],
        compiler_params=pltpu.CompilerParams(vmem_limit_bytes=12 << 20),
        name="finish",
    )(*given)


def solution(mesh):
    spec = P(None, ("layer", "head"), None)
    return jax.shard_map(
        shards, mesh=mesh, in_specs=(spec,) * 3, out_specs=(spec,) * 2, check_vma=False
    )
```

```python
import functools
import math

import jax
import jax.numpy as jnp
from jax import lax
from jax.experimental import pallas as pl
from jax.experimental.pallas import tpu as pltpu
from jax.sharding import PartitionSpec as P

NS_ITERS = 5
quintic_a = 3.4445
quintic_b = -4.775
quintic_c = 2.0315
norm_epsilon = 1e-07
momentum_decay = 0.95

bf16 = jnp.bfloat16
f32 = jnp.float32
MESH = pl.DeviceIdType.MESH
LAYERS, ROWS, LATENT = 4, 256, 512
ALL_ROWS = 32768
T = 128
BLOCKS = [(i, j) for i in range(4) for j in range(i, 4)]
HALF = len(BLOCKS) * T // 2
PIECE = HALF // 16
CHUNK = 64
OFFSETS = [(1, 1, 2), (1, 1, 0), (1, 0, 2)]
OFFSETS += [(1, j, z) for z in (1, 3) for j in (0, 1)] + [(1, 0, 0)]
OFFSETS += [(0, 1, 2)] + [(0, j, z) for z in (1, 3) for j in (0, 1)]
OFFSETS += [(0, 1, 0), (0, 0, 2)]


def split(x):
    high = x.astype(bf16)
    return high, (x - high.astype(f32)).astype(bf16)


def dot(x, y):
    return jnp.dot(x, y, preferred_element_type=f32)


def dot3(x, y):
    return dot(x[0], y[0]) + (dot(x[0], y[1]) + dot(x[1], y[0]))


def mm(x, y):
    return dot3(x, y)


def mm_even(x, y):
    h = x[0].shape[0] // 2
    top = dot3([t[:h] for t in x], y)
    low = dot3([t[h:] for t in x], [t[:, h:] for t in y])
    return jnp.concatenate([top, jnp.concatenate([top[:, h:].T, low], 1)], 0)


def square_even(x):
    high, low = x
    h = high.shape[0] // 2
    cross = dot(high, low)
    top, last = dot(high[:h], high), dot(high[h:], high[:, h:])
    first = top[:, :h] + (cross[:h, :h] + cross[:h, :h].T)
    side = top[:, h:] + (cross[:h, h:] + cross[h:, :h].T)
    last = last + (cross[h:, h:] + cross[h:, h:].T)
    return jnp.concatenate(
        [jnp.concatenate([first, side], 1), jnp.concatenate([side.T, last], 1)], 0)


def eye(n):
    rows = lax.broadcasted_iota(jnp.int32, (n, n), 0)
    return rows == lax.broadcasted_iota(jnp.int32, (n, n), 1)


def layer_polynomial(gram, scratch, start):
    n = gram.shape[0]
    diag = jnp.where(eye(gram.shape[0]), f32(quintic_a), f32(0.0))
    s, q = gram, None
    for k in range(NS_ITERS):
        part = split(s)
        m = diag + (quintic_b * s + quintic_c * square_even(part))
        if k == 0:
            scratch[...] = m
        ms = split(m)
        if k < NS_ITERS - 1:
            s = mm_even(split(mm_even(part, ms)), ms)
        q = scratch[pl.ds(start, n // 2), :] if k == 0 else dot3(split(q), ms)
    return q


def polynomials(grams, product):
    n = grams[0].shape[0]
    diag = jnp.where(eye(n), f32(quintic_a), f32(0.0))
    s, q = list(grams), [None] * len(grams)
    for k in range(NS_ITERS):
        parts = [split(t) for t in s]
        m = [
            diag + (quintic_b * t + quintic_c * product(u, u)) for t, u in zip(s, parts)
        ]
        ms = [split(t) for t in m]
        if k < NS_ITERS - 1:
            r = [split(product(u, v)) for u, v in zip(parts, ms)]
            s = [product(u, v) for u, v in zip(r, ms)]
        q = m if k == 0 else [product(split(u), v) for u, v in zip(q, ms)]
    return q


def unpacked(blocks):
    tiles = {}
    for b, (i, j) in enumerate(BLOCKS):
        v = blocks[b * T:(b + 1) * T, :]
        tiles[i, j] = v
        if i != j:
            tiles[j, i] = v.T
    return jnp.concatenate(
        [jnp.concatenate([tiles[i, j] for j in range(4)], 1) for i in range(4)], 0)


def trace(x):
    return jnp.sum(jnp.where(eye(x.shape[0]), x, f32(0.0)))


def exchange(
    m_hbm, g1_hbm, g2_hbm, o1_ref, own2_ref, got,
    ins, y1_ref, y2_ref, q1_ref, rx, rx2, mate, tx, stage, part, core_in, own, rs, gath,
    q_full, q2_ref, rounds,
    s_in, s_row, r_row, s_core, r_core, s_rs, r_rs, s_ag, r_ag, s_rel, r_rel,
    s_q, r_q, s_mate, r_mate, s_own, r_own,
):
    x = lax.axis_index("layer")
    head = lax.axis_index("head")
    y, z, c = head // 8, (head // 2) % 4, head % 2
    b0, b1 = (x + z) % 2, (y + z) % 2
    lay = b0 + 2 * b1
    lays = [(1 - b0) + 2 * b1, b0 + 2 * (1 - b1), (1 - b0) + 2 * (1 - b1)]
    i, j = x // 2, y // 2
    t = (i * 2 + j) * 4 + z

    def at(x, y, z, c):
        return (x, (y * 4 + z) * 2 + c)

    steps = []
    for a in range(3):
        for s in range(2):
            d = 1 if s == 0 else 3
            steps.append(((x + d) % 4 if a == 0 else x, (y + d) % 4 if a == 1 else y,
                          (z + d) % 4 if a == 2 else z))
    team = []
    for di, dj, dz in OFFSETS:
        i2, j2, z2 = (i + di) % 2, (j + dj) % 2, (z + dz) % 4
        team.append(((2 * i2 + (b0 + z2) % 2, 2 * j2 + (b1 + z2) % 2, z2),
                     (i2 * 2 + j2) * 4 + z2))
    partner = at(x, y, z, 1 - c)
    always = x < 4

    def phase(name):
        def run(body):
            with jax.named_scope(name):
                pl.when(always)(body)
        return run


    barrier = pltpu.get_barrier_semaphore()
    greet = [partner]
    greet += [at(*p, k) for p in steps for k in (c, 1 - c)]
    for who in greet:
        pl.semaphore_signal(barrier, inc=1, device_id=who, device_id_type=MESH)

    turn = lays + [lay]
    loads = [
        [pltpu.make_async_copy(h.at[n], ins.at[k, w], s_in.at[k, w])
         for k, h in enumerate((m_hbm, g1_hbm, g2_hbm))]
        for w, n in enumerate(turn)
    ]
    for group in loads:
        for copy in group:
            copy.start()
    def send(src, dst, ss, rr, who):
        return pltpu.make_async_remote_copy(
            src_ref=src, dst_ref=dst, send_sem=ss, recv_sem=rr, device_id=who,
            device_id_type=MESH)

    row_copies = [
        [send(y2_ref.at[lays[k // 2], pl.ds((k % 2) * 128 + h * CHUNK, CHUNK), :],
              rx.at[h, pl.ds(k * CHUNK, CHUNK), :], s_row.at[h, k], r_row.at[h, k], at(*p, c))
         for k, p in enumerate(steps)]
        for h in range(2)
    ]

    near = [at(*p, c) for p in steps]
    far = [at((x + 2) % 4, y, z, c), at(x, (y + 2) % 4, z, c), at(x, y, (z + 2) % 4, c)]
    told = [near, near + far, far[:1]]

    def tell(k):
        for who in told[k]:
            pl.semaphore_signal(rounds.at[k], inc=1, device_id=who, device_id_type=MESH)

    @phase("w_barrier")
    def _():
        pl.semaphore_wait(barrier, len(greet))
        tell(0)

    for w, n in enumerate(turn):
        @phase("p01")
        def _(w=w, n=n):
            for copy in loads[w]:
                copy.wait()
            one = (momentum_decay * ins[0, w].astype(f32) + ins[1, w].astype(f32)).astype(bf16)
            y1_ref[n] = one
            y2_ref[n] = (momentum_decay * one.astype(f32) + ins[2, w].astype(f32)).astype(bf16)

        if w < 3:
            for h in range(2):
                for k in (2 * w, 2 * w + 1):
                    row_copies[h][k].start()

    @phase("w_tell")
    def _():
        pl.semaphore_wait(rounds.at[0], len(told[0]))
        tell(1)

    def heads(ns):
        grams = []
        norms = []
        for n in ns:
            v = y1_ref[n]
            g = lax.dot_general(v, v, (((1,), (1,)), ((), ())), preferred_element_type=f32)
            norm = jnp.sqrt(trace(g)) + norm_epsilon
            grams.append(g * (1.0 / (norm * norm)))
            norms.append(norm)
        for n, q, norm in zip(ns, polynomials(grams, mm), norms):
            high, low = split(q * (math.sqrt(max(ROWS, LATENT)) / norm))
            q1_ref[n, 0] = high
            q1_ref[n, 1] = low

    def gram_of(views, first):
        for i4 in range(4):
            total = None
            for v in views:
                g = lax.dot_general(
                    v[:, pl.ds(i4 * T, T)], v[:, pl.ds(i4 * T, LATENT - i4 * T)],
                    (((0,), (0,)), ((), ())), preferred_element_type=f32)
                total = g if total is None else total + g
            for j4 in range(i4, 4):
                rows = pl.ds(BLOCKS.index((i4, j4)) * T, T)
                value = total[:, (j4 - i4) * T:(j4 - i4 + 1) * T]
                part[rows, :] = value if first else part[rows, :] + value

    @phase("w_rows0")
    def _():
        for copy in row_copies[0]:
            copy.wait()

    @phase("p02")
    def _():
        gram_of([y2_ref.at[lay], rx.at[0]], True)

    @phase("w_rows1")
    def _():
        pl.semaphore_wait(rounds.at[1], len(told[1]))
        tell(2)
        for copy in row_copies[1]:
            copy.wait()

    @phase("p03")
    def _():
        gram_of([rx.at[1]], False)

    theirs = pl.ds(pl.multiple_of((1 - c) * HALF, 8), HALF)
    mine = pl.ds(pl.multiple_of(c * HALF, 8), HALF)
    def section(core, side):
        return pl.ds(pl.multiple_of(core * HALF + side * (HALF // 2), 8), HALF // 2)

    sides = [1 - i, i]
    swaps = [
        send(part.at[section(1 - c, side), :], core_in.at[section(0, side), :], s_core.at[k],
             r_core.at[k], partner)
        for k, side in enumerate(sides)
    ]
    rs_copies = []
    for k, (p, t2) in enumerate(team):
        rs_copies.append(send(
            own.at[pl.ds(pl.multiple_of(t2 * PIECE, 8), PIECE), :], rs.at[k],
            s_rs.at[k], r_rs.at[k], at(*p, c)))
    mates = [send(rx, rx2, s_mate.at[0], r_mate.at[0], partner),
             send(y2_ref.at[lay], mate, s_mate.at[1], r_mate.at[1], partner)]
    for copy in swaps:
        copy.start()

    @phase("w_swap")
    def _():
        pl.semaphore_wait(rounds.at[2], len(told[2]))
        for k, side in enumerate(sides):
            swaps[k].wait()
            own[section(0, side), :] = part[section(c, side), :] + core_in[section(0, side), :]
            for copy in (rs_copies[:8] if k == 0 else rs_copies[8:]):
                copy.start()
        for copy in mates:
            copy.start()

    @phase("p04")
    def _():
        heads((0, 1))

    @phase("w_rs")
    def _():
        for copy in rs_copies:
            copy.wait()

    total = own[pl.ds(pl.multiple_of(t * PIECE, 8), PIECE), :]
    for k in range(15):
        total = total + rs[k]
    here = pl.ds(pl.multiple_of(c * HALF + t * PIECE, 8), PIECE)
    gath[here, :] = total
    ag_copies = [
        send(gath.at[here, :], gath.at[here, :], s_ag.at[k], r_ag.at[k], at(*p, c))
        for k, (p, _) in enumerate(team)
    ]
    for copy in ag_copies:
        copy.start()
    @phase("p05")
    def _():
        heads((2, 3))

    def relay(k, t3, core):
        there = pl.ds(pl.multiple_of(core * HALF + t3 * PIECE, 8), PIECE)
        return send(gath.at[there, :], gath.at[there, :], s_rel.at[k], r_rel.at[k], partner)

    relays = [(15, t)]
    for k, (di, dj, dz) in enumerate(OFFSETS):
        relays.append((k, (((i + di) % 2) * 2 + (j + dj) % 2) * 4 + (z + 4 - dz) % 4))
    @phase("w_ag")
    def _():
        for k, t3 in [relays[0]] + relays[:0:-1]:
            if k < 15:
                there = pl.ds(pl.multiple_of(c * HALF + t3 * PIECE, 8), PIECE)
                send(gath.at[there, :], gath.at[there, :], s_ag.at[k], r_ag.at[k],
                     at(*team[k][0], c)).wait_recv()
            relay(k, t3, c).start()

    @phase("w_relay")
    def _():
        for copy in ag_copies:
            copy.wait_send()
        for k, t3 in relays:
            relay(k, t3, c).wait_send()
        for k, t3 in relays:
            relay(k, t3, 1 - c).wait_recv()

    @phase("p06")
    def _():
        gram = unpacked(gath[...])
        norm = jnp.sqrt(trace(gram)) + norm_epsilon
        q = layer_polynomial(
            gram * (1.0 / (norm * norm)), q_full, pl.multiple_of(c * 256, 256))
        q2_ref[0], q2_ref[1] = split((q * (math.sqrt(ALL_ROWS) / norm)).T)

    def columns(core):
        return pl.ds(pl.multiple_of(core * 256, 256), 256)

    def returned(h, k, d, core):
        return send(
            tx.at[h, d, pl.ds(k * CHUNK, CHUNK), :],
            got.at[k // 2, pl.ds((k % 2) * 128 + h * CHUNK, CHUNK), columns(core)],
            s_q.at[h, k, d], r_q.at[h, k, core], at(*steps[k ^ 1], c if d == 0 else 1 - c))

    for copy in mates:
        copy.wait()
    back = []
    for h in range(2):
        @phase("p07")
        def _(h=h):
            for d, rows in enumerate((rx, rx2)):
                w = rows[h]
                tx[h, d] = (dot(w, q2_ref[0]) + dot(w, q2_ref[1])).astype(bf16)

        for k in range(6):
            for d in range(2):
                back.append(returned(h, k, d, c))
                back[-1].start()

    @phase("p08")
    def _():
        w = mate[...]
        stage[...] = dot(w, q2_ref[0]) + dot(w, q2_ref[1])

    over = [send(stage, own2_ref.at[:, columns(k)], s_own, r_own, partner) for k in (c, 1 - c)]
    over[0].start()

    @phase("p09")
    def _():
        w = y2_ref[lay]
        own2_ref[:, columns(c)] = dot(w, q2_ref[0]) + dot(w, q2_ref[1])
        for n in range(LAYERS):
            v = y1_ref[n]
            o1_ref[n] = dot(q1_ref[n, 0], v) + dot(q1_ref[n, 1], v)

    @phase("w_back")
    def _():
        over[0].wait_send()
        over[1].wait_recv()
        for copy in back:
            copy.wait_send()
        for h in range(2):
            for k in range(6):
                for core in range(2):
                    returned(h, k, 0, core).wait_recv()


def finish(o1_ref, own2_ref, got, out1, out2, buf, sems):
    x = lax.axis_index("layer")
    head = lax.axis_index("head")
    y, z = head // 8, (head // 2) % 4
    b0, b1 = (x + z) % 2, (y + z) % 2
    copies = [pltpu.make_async_copy(
        own2_ref, out2.at[b0 + 2 * b1], sems.at[LAYERS])]
    for n in range(LAYERS):
        copies.append(pltpu.make_async_copy(o1_ref.at[n], out1.at[n], sems.at[n]))
    for copy in copies:
        copy.start()
    lays = [(1 - b0) + 2 * b1, b0 + 2 * (1 - b1), (1 - b0) + 2 * (1 - b1)]
    for a in range(3):
        buf[a] = got[a].astype(f32)
        copies.append(pltpu.make_async_copy(buf.at[a], out2.at[lays[a]], sems.at[LAYERS + 1 + a]))
        copies[-1].start()
    for copy in copies:
        copy.wait()


def shards(momentum, grad_one, grad_two):
    vmem = pl.BlockSpec(memory_space=pltpu.VMEM)
    hbm = pl.BlockSpec(memory_space=pltpu.MemorySpace.HBM)
    dma = pltpu.SemaphoreType.DMA
    given = pl.pallas_call(
        exchange,
        out_shape=(
            jax.ShapeDtypeStruct((LAYERS, ROWS, LATENT), f32),
            jax.ShapeDtypeStruct((ROWS, LATENT), f32),
            jax.ShapeDtypeStruct((3, ROWS, LATENT), bf16),
        ),
        in_specs=[hbm] * 3,
        out_specs=(vmem,) * 3,
        scratch_shapes=[
            pltpu.VMEM((3, LAYERS, ROWS, LATENT), bf16),
            pltpu.VMEM((LAYERS, ROWS, LATENT), bf16),
            pltpu.VMEM((LAYERS, ROWS, LATENT), bf16),
            pltpu.VMEM((LAYERS, 2, ROWS, ROWS), bf16),
            pltpu.VMEM((2, 6 * CHUNK, LATENT), bf16),
            pltpu.VMEM((2, 6 * CHUNK, LATENT), bf16),
            pltpu.VMEM((ROWS, LATENT), bf16),
            pltpu.VMEM((2, 2, 6 * CHUNK, LATENT // 2), bf16),
            pltpu.VMEM((ROWS, LATENT // 2), f32),
            pltpu.VMEM((2 * HALF, T), f32),
            pltpu.VMEM((HALF, T), f32),
            pltpu.VMEM((HALF, T), f32),
            pltpu.VMEM((15, PIECE, T), f32),
            pltpu.VMEM((2 * HALF, T), f32),
            pltpu.VMEM((LATENT, LATENT), f32),
            pltpu.VMEM((2, LATENT, LATENT // 2), bf16),
            pltpu.SemaphoreType.REGULAR((3,)),
            dma((3, LAYERS)), dma((2, 6)), dma((2, 6)), dma((2,)), dma((2,)),
            dma((15,)), dma((15,)), dma((15,)), dma((15,)), dma((16,)), dma((16,)),
            dma((2, 6, 2)), dma((2, 6, 2)), dma((2,)), dma((2,)), dma, dma,
        ],
        compiler_params=pltpu.CompilerParams(
            collective_id=0, has_side_effects=True, vmem_limit_bytes=32 << 20),
        name="exchange",
    )(*[
        pltpu.with_memory_space_constraint(v, pltpu.MemorySpace.HBM)
        for v in (momentum, grad_one, grad_two)
    ])
    return pl.pallas_call(
        finish,
        out_shape=(jax.ShapeDtypeStruct((LAYERS, ROWS, LATENT), f32),) * 2,
        in_specs=[vmem] * 3,
        out_specs=(hbm,) * 2,
        scratch_shapes=[pltpu.VMEM((3, ROWS, LATENT), f32), dma((LAYERS + 4,))],
        compiler_params=pltpu.CompilerParams(vmem_limit_bytes=12 << 20),
        name="finish",
    )(*given)


def solution(mesh):
    spec = P(None, ("layer", "head"), None)
    return jax.shard_map(
        shards, mesh=mesh, in_specs=(spec,) * 3, out_specs=(spec,) * 2, check_vma=False
    )
```

```python
import functools
import math

import jax
import jax.numpy as jnp
from jax import lax
from jax.experimental import pallas as pl
from jax.experimental.pallas import tpu as pltpu
from jax.sharding import PartitionSpec as P

NS_ITERS = 5
quintic_a = 3.4445
quintic_b = -4.775
quintic_c = 2.0315
norm_epsilon = 1e-07
momentum_decay = 0.95

bf16 = jnp.bfloat16
f32 = jnp.float32
MESH = pl.DeviceIdType.MESH
LAYERS, ROWS, LATENT = 4, 256, 512
ALL_ROWS = 32768
T = 128
BLOCKS = [(i, j) for i in range(4) for j in range(i, 4)]
HALF = len(BLOCKS) * T // 2
PIECE = HALF // 16
CHUNK = 64
OFFSETS = [(1, 1, 2), (1, 1, 0), (1, 0, 2)]
OFFSETS += [(1, j, z) for z in (1, 3) for j in (0, 1)] + [(1, 0, 0)]
OFFSETS += [(0, 1, 2)] + [(0, j, z) for z in (1, 3) for j in (0, 1)]
OFFSETS += [(0, 1, 0), (0, 0, 2)]
FAR = [0, 1, 2, 8]


def split(x):
    high = x.astype(bf16)
    return high, (x - high.astype(f32)).astype(bf16)


def dot(x, y):
    return jnp.dot(x, y, preferred_element_type=f32)


def dot3(x, y):
    return dot(x[0], y[0]) + (dot(x[0], y[1]) + dot(x[1], y[0]))


def mm(x, y):
    return dot3(x, y)


def mm_even(x, y):
    h = x[0].shape[0] // 2
    top = dot3([t[:h] for t in x], y)
    low = dot3([t[h:] for t in x], [t[:, h:] for t in y])
    return jnp.concatenate([top, jnp.concatenate([top[:, h:].T, low], 1)], 0)


def square_even(x):
    high, low = x
    h = high.shape[0] // 2
    cross = dot(high, low)
    top, last = dot(high[:h], high), dot(high[h:], high[:, h:])
    first = top[:, :h] + (cross[:h, :h] + cross[:h, :h].T)
    side = top[:, h:] + (cross[:h, h:] + cross[h:, :h].T)
    last = last + (cross[h:, h:] + cross[h:, h:].T)
    return jnp.concatenate(
        [jnp.concatenate([first, side], 1), jnp.concatenate([side.T, last], 1)], 0)


def eye(n):
    rows = lax.broadcasted_iota(jnp.int32, (n, n), 0)
    return rows == lax.broadcasted_iota(jnp.int32, (n, n), 1)


def layer_polynomial(gram, scratch, start):
    n = gram.shape[0]
    diag = jnp.where(eye(gram.shape[0]), f32(quintic_a), f32(0.0))
    s, q = gram, None
    for k in range(NS_ITERS):
        part = split(s)
        m = diag + (quintic_b * s + quintic_c * square_even(part))
        if k == 0:
            scratch[...] = m
        ms = split(m)
        if k < NS_ITERS - 1:
            s = mm_even(split(mm_even(part, ms)), ms)
        q = scratch[pl.ds(start, n // 2), :] if k == 0 else dot3(split(q), ms)
    return q


def polynomials(grams, product):
    n = grams[0].shape[0]
    diag = jnp.where(eye(n), f32(quintic_a), f32(0.0))
    s, q = list(grams), [None] * len(grams)
    for k in range(NS_ITERS):
        parts = [split(t) for t in s]
        m = [
            diag + (quintic_b * t + quintic_c * product(u, u)) for t, u in zip(s, parts)
        ]
        ms = [split(t) for t in m]
        if k < NS_ITERS - 1:
            r = [split(product(u, v)) for u, v in zip(parts, ms)]
            s = [product(u, v) for u, v in zip(r, ms)]
        q = m if k == 0 else [product(split(u), v) for u, v in zip(q, ms)]
    return q


def unpacked(blocks):
    tiles = {}
    for b, (i, j) in enumerate(BLOCKS):
        v = blocks[b * T:(b + 1) * T, :]
        tiles[i, j] = v
        if i != j:
            tiles[j, i] = v.T
    return jnp.concatenate(
        [jnp.concatenate([tiles[i, j] for j in range(4)], 1) for i in range(4)], 0)


def trace(x):
    return jnp.sum(jnp.where(eye(x.shape[0]), x, f32(0.0)))


def exchange(
    m_hbm, g1_hbm, g2_hbm, o1_ref, own2_ref, got,
    ins, y1_ref, y2_ref, q1_ref, rx, rx2, mate, tx, stage, part, core_in, own, rs, gath,
    q_full, q2_ref, rounds,
    s_in, s_row, r_row, s_core, r_core, s_rs, r_rs, s_ag, r_ag, s_rel, r_rel,
    s_q, r_q, s_mate, r_mate, s_own, r_own,
):
    x = lax.axis_index("layer")
    head = lax.axis_index("head")
    y, z, c = head // 8, (head // 2) % 4, head % 2
    b0, b1 = (x + z) % 2, (y + z) % 2
    lay = b0 + 2 * b1
    lays = [(1 - b0) + 2 * b1, b0 + 2 * (1 - b1), (1 - b0) + 2 * (1 - b1)]
    i, j = x // 2, y // 2
    t = (i * 2 + j) * 4 + z

    def at(x, y, z, c):
        return (x, (y * 4 + z) * 2 + c)

    steps = []
    for a in range(3):
        for s in range(2):
            d = 1 if s == 0 else 3
            steps.append(((x + d) % 4 if a == 0 else x, (y + d) % 4 if a == 1 else y,
                          (z + d) % 4 if a == 2 else z))
    team = []
    for di, dj, dz in OFFSETS:
        i2, j2, z2 = (i + di) % 2, (j + dj) % 2, (z + dz) % 4
        team.append(((2 * i2 + (b0 + z2) % 2, 2 * j2 + (b1 + z2) % 2, z2),
                     (i2 * 2 + j2) * 4 + z2))
    partner = at(x, y, z, 1 - c)
    always = x < 4

    def phase(name):
        def run(body):
            with jax.named_scope(name):
                pl.when(always)(body)
        return run


    turn = lays + [lay]
    loads = [
        [pltpu.make_async_copy(h.at[n], ins.at[k, w], s_in.at[w])
         for k, h in enumerate((m_hbm, g1_hbm, g2_hbm))]
        for w, n in enumerate(turn)
    ]
    for copy in loads[0]:
        copy.start()
    barrier = pltpu.get_barrier_semaphore()
    greet = [partner]
    greet += [at(*p, k) for p in steps for k in (c, 1 - c)]
    for who in greet:
        pl.semaphore_signal(barrier, inc=1, device_id=who, device_id_type=MESH)

    for group in loads[1:]:
        for copy in group:
            copy.start()
    def send(src, dst, ss, rr, who):
        return pltpu.make_async_remote_copy(
            src_ref=src, dst_ref=dst, send_sem=ss, recv_sem=rr, device_id=who,
            device_id_type=MESH)

    row_copies = [
        [send(y2_ref.at[lays[k // 2], pl.ds((k % 2) * 128 + h * CHUNK, CHUNK), :],
              rx.at[h, pl.ds(k * CHUNK, CHUNK), :], s_row.at[h], r_row.at[h], at(*p, c))
         for k, p in enumerate(steps)]
        for h in range(2)
    ]

    near = [at(*p, c) for p in steps]
    far = [at((x + 2) % 4, y, z, c), at(x, (y + 2) % 4, z, c), at(x, y, (z + 2) % 4, c)]
    told = [near, near + far, far[:1]]

    def tell(k):
        for who in told[k]:
            pl.semaphore_signal(rounds.at[k], inc=1, device_id=who, device_id_type=MESH)

    @phase("w_barrier")
    def _():
        pl.semaphore_wait(barrier, len(greet))
        tell(0)

    def loaded(w):
        pltpu.make_async_copy(ins.at[:, w], ins.at[:, w], s_in.at[w]).wait()

    def momentum(w, n, starts, rows):
        for first in starts:
            r = pl.ds(first, rows)
            one = momentum_decay * ins[0, w, r, :].astype(f32) + ins[1, w, r, :].astype(f32)
            one = one.astype(bf16)
            y1_ref[n, r, :] = one
            two = momentum_decay * one.astype(f32) + ins[2, w, r, :].astype(f32)
            y2_ref[n, r, :] = two.astype(bf16)

    for h in range(2):
        for w in range(3):
            @phase("p01")
            def _(h=h, w=w):
                if h == 0:
                    loaded(w)
                momentum(w, turn[w], (h * CHUNK, 128 + h * CHUNK), CHUNK)

            for k in (2 * w, 2 * w + 1):
                row_copies[h][k].start()

    @phase("p01o")
    def _():
        loaded(3)
        momentum(3, lay, (0,), ROWS)

    @phase("w_tell")
    def _():
        pl.semaphore_wait(rounds.at[0], len(told[0]))
        tell(1)

    def heads(ns):
        grams = []
        norms = []
        for n in ns:
            v = y1_ref[n]
            g = lax.dot_general(v, v, (((1,), (1,)), ((), ())), preferred_element_type=f32)
            norm = jnp.sqrt(trace(g)) + norm_epsilon
            grams.append(g * (1.0 / (norm * norm)))
            norms.append(norm)
        for n, q, norm in zip(ns, polynomials(grams, mm), norms):
            high, low = split(q * (math.sqrt(max(ROWS, LATENT)) / norm))
            q1_ref[n, 0] = high
            q1_ref[n, 1] = low

    def gram_of(views, first):
        for i4 in range(4):
            total = None
            for v in views:
                g = lax.dot_general(
                    v[:, pl.ds(i4 * T, T)], v[:, pl.ds(i4 * T, LATENT - i4 * T)],
                    (((0,), (0,)), ((), ())), preferred_element_type=f32)
                total = g if total is None else total + g
            for j4 in range(i4, 4):
                rows = pl.ds(BLOCKS.index((i4, j4)) * T, T)
                value = total[:, (j4 - i4) * T:(j4 - i4 + 1) * T]
                part[rows, :] = value if first else part[rows, :] + value

    @phase("p_own")
    def _():
        gram_of([y2_ref.at[lay]], True)

    @phase("w_rows0")
    def _():
        send(rx.at[0], rx.at[0], s_row.at[0], r_row.at[0], partner).wait()

    @phase("p02")
    def _():
        gram_of([rx.at[0]], False)

    @phase("w_rows1")
    def _():
        pl.semaphore_wait(rounds.at[1], len(told[1]))
        tell(2)
        send(rx.at[1], rx.at[1], s_row.at[1], r_row.at[1], partner).wait()

    @phase("p03")
    def _():
        gram_of([rx.at[1]], False)

    theirs = pl.ds(pl.multiple_of((1 - c) * HALF, 8), HALF)
    mine = pl.ds(pl.multiple_of(c * HALF, 8), HALF)
    def section(core, side):
        return pl.ds(pl.multiple_of(core * HALF + side * (HALF // 2), 8), HALF // 2)

    sides = [1 - i, i]
    swaps = [
        send(part.at[section(1 - c, side), :], core_in.at[section(0, side), :], s_core.at[k],
             r_core.at[k], partner)
        for k, side in enumerate(sides)
    ]
    rs_copies = []
    for k, (p, t2) in enumerate(team):
        rs_copies.append(send(
            own.at[pl.ds(pl.multiple_of(t2 * PIECE, 8), PIECE), :], rs.at[k],
            s_rs, r_rs, at(*p, c)))
    mates = [send(rx, rx2, s_mate.at[0], r_mate.at[0], partner),
             send(y2_ref.at[lay], mate, s_mate.at[1], r_mate.at[1], partner)]
    for copy in swaps:
        copy.start()

    @phase("w_swap")
    def _():
        pl.semaphore_wait(rounds.at[2], len(told[2]))
        for k, side in enumerate(sides):
            swaps[k].wait()
            own[section(0, side), :] = part[section(c, side), :] + core_in[section(0, side), :]
            for copy in (rs_copies[:8] if k == 0 else rs_copies[8:]):
                copy.start()
        for copy in mates:
            copy.start()

    @phase("p04")
    def _():
        heads((0, 1))

    @phase("w_rs")
    def _():
        send(rs, rs, s_rs, r_rs, partner).wait()

    total = own[pl.ds(pl.multiple_of(t * PIECE, 8), PIECE), :]
    for k in range(15):
        total = total + rs[k]
    here = pl.ds(pl.multiple_of(c * HALF + t * PIECE, 8), PIECE)
    gath[here, :] = total
    ag_copies = [
        send(gath.at[here, :], gath.at[here, :], s_ag, r_ag.at[int(k in FAR)], at(*p, c))
        for k, (p, _) in enumerate(team)
    ]
    for copy in ag_copies:
        copy.start()

    @phase("p05")
    def _():
        heads((2, 3))

    def relay(k, t3, core):
        there = pl.ds(pl.multiple_of(core * HALF + t3 * PIECE, 8), PIECE)
        return send(gath.at[there, :], gath.at[there, :], s_rel, r_rel, partner)

    relays = [(15, t)]
    for k, (di, dj, dz) in enumerate(OFFSETS):
        relays.append((k, (((i + di) % 2) * 2 + (j + dj) % 2) * 4 + (z + 4 - dz) % 4))
    @phase("w_ag")
    def _():
        relay(*relays[0], c).start()
        for group in range(2):
            ks = [k for k in range(15) if (k in FAR) == (group == 1)]
            some = rs.at[pl.ds(0, len(ks))]
            send(some, some, s_ag, r_ag.at[group], partner).wait_recv()
            for k in ks:
                relay(*relays[k + 1], c).start()

    @phase("w_relay")
    def _():
        send(rs, rs, s_ag, r_ag.at[0], partner).wait_send()
        send(gath.at[mine, :], gath.at[mine, :], s_rel, r_rel, partner).wait_send()
        send(gath.at[theirs, :], gath.at[theirs, :], s_rel, r_rel, partner).wait_recv()

    @phase("p06")
    def _():
        gram = unpacked(gath[...])
        norm = jnp.sqrt(sum(trace(gram[k:k + T, k:k + T]) for k in range(0, LATENT, T)))
        norm = norm + norm_epsilon
        q = layer_polynomial(
            gram * (1.0 / (norm * norm)), q_full, pl.multiple_of(c * 256, 256))
        q2_ref[0], q2_ref[1] = split((q * (math.sqrt(ALL_ROWS) / norm)).T)

    def columns(core):
        return pl.ds(pl.multiple_of(core * 256, 256), 256)

    def returned(h, k, d, core):
        return send(
            tx.at[h, d, pl.ds(k * CHUNK, CHUNK), :],
            got.at[k // 2, pl.ds((k % 2) * 128 + h * CHUNK, CHUNK), columns(core)],
            s_q, r_q, at(*steps[k ^ 1], c if d == 0 else 1 - c))

    for copy in mates:
        copy.wait()
    back = []
    for h in range(2):
        @phase("p07")
        def _(h=h):
            for d, rows in enumerate((rx, rx2)):
                w = rows[h]
                tx[h, d] = (dot(w, q2_ref[0]) + dot(w, q2_ref[1])).astype(bf16)

        for k in range(6):
            for d in range(2):
                back.append(returned(h, k, d, c))
                back[-1].start()

    @phase("p08")
    def _():
        w = mate[...]
        stage[...] = dot(w, q2_ref[0]) + dot(w, q2_ref[1])

    over = [send(stage, own2_ref.at[:, columns(k)], s_own, r_own, partner) for k in (c, 1 - c)]
    over[0].start()

    @phase("p09")
    def _():
        w = y2_ref[lay]
        own2_ref[:, columns(c)] = dot(w, q2_ref[0]) + dot(w, q2_ref[1])
        for n in range(LAYERS):
            v = y1_ref[n]
            o1_ref[n] = dot(q1_ref[n, 0], v) + dot(q1_ref[n, 1], v)

    @phase("w_back")
    def _():
        over[0].wait_send()
        over[1].wait_recv()
        send(got, got, s_q, r_q, partner).wait()


def finish(o1_ref, own2_ref, got, out1, out2, buf, sems):
    x = lax.axis_index("layer")
    head = lax.axis_index("head")
    y, z = head // 8, (head // 2) % 4
    b0, b1 = (x + z) % 2, (y + z) % 2
    copies = [pltpu.make_async_copy(
        own2_ref, out2.at[b0 + 2 * b1], sems.at[LAYERS])]
    for n in range(LAYERS):
        copies.append(pltpu.make_async_copy(o1_ref.at[n], out1.at[n], sems.at[n]))
    for copy in copies:
        copy.start()
    lays = [(1 - b0) + 2 * b1, b0 + 2 * (1 - b1), (1 - b0) + 2 * (1 - b1)]
    for a in range(3):
        buf[a] = got[a].astype(f32)
        copies.append(pltpu.make_async_copy(buf.at[a], out2.at[lays[a]], sems.at[LAYERS + 1 + a]))
        copies[-1].start()
    for copy in copies:
        copy.wait()


def shards(momentum, grad_one, grad_two):
    vmem = pl.BlockSpec(memory_space=pltpu.VMEM)
    hbm = pl.BlockSpec(memory_space=pltpu.MemorySpace.HBM)
    dma = pltpu.SemaphoreType.DMA
    given = pl.pallas_call(
        exchange,
        out_shape=(
            jax.ShapeDtypeStruct((LAYERS, ROWS, LATENT), f32),
            jax.ShapeDtypeStruct((ROWS, LATENT), f32),
            jax.ShapeDtypeStruct((3, ROWS, LATENT), bf16),
        ),
        in_specs=[hbm] * 3,
        out_specs=(vmem,) * 3,
        scratch_shapes=[
            pltpu.VMEM((3, LAYERS, ROWS, LATENT), bf16),
            pltpu.VMEM((LAYERS, ROWS, LATENT), bf16),
            pltpu.VMEM((LAYERS, ROWS, LATENT), bf16),
            pltpu.VMEM((LAYERS, 2, ROWS, ROWS), bf16),
            pltpu.VMEM((2, 6 * CHUNK, LATENT), bf16),
            pltpu.VMEM((2, 6 * CHUNK, LATENT), bf16),
            pltpu.VMEM((ROWS, LATENT), bf16),
            pltpu.VMEM((2, 2, 6 * CHUNK, LATENT // 2), bf16),
            pltpu.VMEM((ROWS, LATENT // 2), f32),
            pltpu.VMEM((2 * HALF, T), f32),
            pltpu.VMEM((HALF, T), f32),
            pltpu.VMEM((HALF, T), f32),
            pltpu.VMEM((15, PIECE, T), f32),
            pltpu.VMEM((2 * HALF, T), f32),
            pltpu.VMEM((LATENT, LATENT), f32),
            pltpu.VMEM((2, LATENT, LATENT // 2), bf16),
            pltpu.SemaphoreType.REGULAR((3,)),
            dma((LAYERS,)), dma((2,)), dma((2,)), dma((2,)), dma((2,)),
            dma, dma, dma, dma((2,)), dma, dma, dma, dma, dma((2,)), dma((2,)), dma, dma,
        ],
        compiler_params=pltpu.CompilerParams(
            collective_id=0, has_side_effects=True, vmem_limit_bytes=32 << 20),
        name="exchange",
    )(*[
        pltpu.with_memory_space_constraint(v, pltpu.MemorySpace.HBM)
        for v in (momentum, grad_one, grad_two)
    ])
    return pl.pallas_call(
        finish,
        out_shape=(jax.ShapeDtypeStruct((LAYERS, ROWS, LATENT), f32),) * 2,
        in_specs=[vmem] * 3,
        out_specs=(hbm,) * 2,
        scratch_shapes=[pltpu.VMEM((3, ROWS, LATENT), f32), dma((LAYERS + 4,))],
        compiler_params=pltpu.CompilerParams(vmem_limit_bytes=12 << 20),
        name="finish",
    )(*given)


def solution(mesh):
    spec = P(None, ("layer", "head"), None)
    return jax.shard_map(
        shards, mesh=mesh, in_specs=(spec,) * 3, out_specs=(spec,) * 2, check_vma=False
    )
```

```python
import functools
import math

import jax
import jax.numpy as jnp
from jax import lax
from jax.experimental import pallas as pl
from jax.experimental.pallas import tpu as pltpu
from jax.sharding import PartitionSpec as P

NS_ITERS = 5
quintic_a = 3.4445
quintic_b = -4.775
quintic_c = 2.0315
norm_epsilon = 1e-07
momentum_decay = 0.95

bf16 = jnp.bfloat16
f32 = jnp.float32
MESH = pl.DeviceIdType.MESH
LAYERS, ROWS, LATENT = 4, 256, 512
ALL_ROWS = 32768
T = 128
BLOCKS = [(i, j) for i in range(4) for j in range(i, 4)]
HALF = len(BLOCKS) * T // 2
PIECE = HALF // 8
CHUNK = 64
OFFSETS = [(1, 1, 2), (1, 1, 0), (1, 0, 2)]
OFFSETS += [(1, j, z) for z in (1, 3) for j in (0, 1)] + [(1, 0, 0)]
OFFSETS += [(0, 1, 2)] + [(0, j, z) for z in (1, 3) for j in (0, 1)]
OFFSETS += [(0, 1, 0), (0, 0, 2)]
FAR = [0, 1, 2, 8]


def split(x):
    high = x.astype(bf16)
    return high, (x - high.astype(f32)).astype(bf16)


def dot(x, y):
    return jnp.dot(x, y, preferred_element_type=f32)


def dot3(x, y):
    return dot(x[0], y[0]) + (dot(x[0], y[1]) + dot(x[1], y[0]))


def mm(x, y):
    return dot3(x, y)


def mm_even(x, y):
    h = x[0].shape[0] // 2
    top = dot3([t[:h] for t in x], y)
    low = dot3([t[h:] for t in x], [t[:, h:] for t in y])
    return jnp.concatenate([top, jnp.concatenate([top[:, h:].T, low], 1)], 0)


def square_even(x):
    high, low = x
    h = high.shape[0] // 2
    cross = dot(high, low)
    top, last = dot(high[:h], high), dot(high[h:], high[:, h:])
    first = top[:, :h] + (cross[:h, :h] + cross[:h, :h].T)
    side = top[:, h:] + (cross[:h, h:] + cross[h:, :h].T)
    last = last + (cross[h:, h:] + cross[h:, h:].T)
    return jnp.concatenate(
        [jnp.concatenate([first, side], 1), jnp.concatenate([side.T, last], 1)], 0)


def eye(n):
    rows = lax.broadcasted_iota(jnp.int32, (n, n), 0)
    return rows == lax.broadcasted_iota(jnp.int32, (n, n), 1)


def layer_polynomial(gram, scratch, start):
    n = gram.shape[0]
    diag = jnp.where(eye(gram.shape[0]), f32(quintic_a), f32(0.0))
    s, q = gram, None
    for k in range(NS_ITERS):
        part = split(s)
        m = diag + (quintic_b * s + quintic_c * square_even(part))
        if k == 0:
            scratch[...] = m
        ms = split(m)
        if k < NS_ITERS - 1:
            s = mm_even(split(mm_even(part, ms)), ms)
        q = scratch[pl.ds(start, n // 2), :] if k == 0 else dot3(split(q), ms)
    return q


def polynomials(grams, product):
    n = grams[0].shape[0]
    diag = jnp.where(eye(n), f32(quintic_a), f32(0.0))
    s, q = list(grams), [None] * len(grams)
    for k in range(NS_ITERS):
        parts = [split(t) for t in s]
        m = [
            diag + (quintic_b * t + quintic_c * product(u, u)) for t, u in zip(s, parts)
        ]
        ms = [split(t) for t in m]
        if k < NS_ITERS - 1:
            r = [split(product(u, v)) for u, v in zip(parts, ms)]
            s = [product(u, v) for u, v in zip(r, ms)]
        q = m if k == 0 else [product(split(u), v) for u, v in zip(q, ms)]
    return q


def unpacked(blocks):
    tiles = {}
    for b, (i, j) in enumerate(BLOCKS):
        v = blocks[b * T:(b + 1) * T, :]
        tiles[i, j] = v
        if i != j:
            tiles[j, i] = v.T
    return jnp.concatenate(
        [jnp.concatenate([tiles[i, j] for j in range(4)], 1) for i in range(4)], 0)


def trace(x):
    return jnp.sum(jnp.where(eye(x.shape[0]), x, f32(0.0)))


def exchange(
    m_hbm, g1_hbm, g2_hbm, o1_ref, own2_ref, got,
    ins, y1_ref, y2_ref, q1_ref, rx, mate, tx, stage, part, rs, gath,
    q_full, q2_ref, rounds,
    s_in, s_row, r_row, s_rs, r_rs, s_ag, r_ag, s_rel, r_rel,
    s_q, r_q, s_mate, r_mate, s_own, r_own,
):
    x = lax.axis_index("layer")
    head = lax.axis_index("head")
    y, z, c = head // 8, (head // 2) % 4, head % 2
    b0, b1 = (x + z) % 2, (y + z) % 2
    lay = b0 + 2 * b1
    lays = [(1 - b0) + 2 * b1, b0 + 2 * (1 - b1), (1 - b0) + 2 * (1 - b1)]
    i, j = x // 2, y // 2
    t = (i * 2 + j) * 4 + z

    def at(x, y, z, c):
        return (x, (y * 4 + z) * 2 + c)

    steps = []
    for a in range(3):
        for s in range(2):
            d = 1 if s == 0 else 3
            steps.append(((x + d) % 4 if a == 0 else x, (y + d) % 4 if a == 1 else y,
                          (z + d) % 4 if a == 2 else z))
    team = []
    for di, dj, dz in OFFSETS:
        i2, j2, z2 = (i + di) % 2, (j + dj) % 2, (z + dz) % 4
        team.append(((2 * i2 + (b0 + z2) % 2, 2 * j2 + (b1 + z2) % 2, z2),
                     (i2 * 2 + j2) * 4 + z2))
    partner = at(x, y, z, 1 - c)
    always = x < 4

    def phase(name, lead=False):
        def run(body):
            with jax.named_scope(name):
                pl.when(c == 1 if lead else always)(body)
        return run


    turn = lays + [lay]
    loads = [
        [pltpu.make_async_copy(h.at[n], ins.at[k, w], s_in.at[w])
         for k, h in enumerate((m_hbm, g1_hbm, g2_hbm))]
        for w, n in enumerate(turn)
    ]
    for copy in loads[0]:
        copy.start()
    barrier = pltpu.get_barrier_semaphore()
    greet = [partner]
    greet += [at(*p, k) for p in steps for k in (c, 1 - c)]
    for who in greet:
        pl.semaphore_signal(barrier, inc=1, device_id=who, device_id_type=MESH)

    for group in loads[1:]:
        for copy in group:
            copy.start()
    def send(src, dst, ss, rr, who):
        return pltpu.make_async_remote_copy(
            src_ref=src, dst_ref=dst, send_sem=ss, recv_sem=rr, device_id=who,
            device_id_type=MESH)

    row_copies = [
        [send(y2_ref.at[lays[k // 2], pl.ds((k % 2) * 128 + h * CHUNK, CHUNK), :],
              rx.at[h, pl.ds(pl.multiple_of((k * 2 + c) * CHUNK, CHUNK), CHUNK), :],
              s_row.at[h], r_row.at[h], at(*p, 1))
         for k, p in enumerate(steps)]
        for h in range(2)
    ]
    mates = [send(y2_ref.at[lay], mate, s_mate.at[0], r_mate.at[0], partner),
             send(rx, rx, s_mate.at[1], r_mate.at[1], partner)]
    near = [at(*p, c) for p in steps]
    far = [at((x + 2) % 4, y, z, c), at(x, (y + 2) % 4, z, c), at(x, y, (z + 2) % 4, c)]
    told = [near, near + far, far[:1]]

    def tell(k):
        for who in told[k]:
            pl.semaphore_signal(rounds.at[k], inc=1, device_id=who, device_id_type=MESH)

    @phase("w_barrier")
    def _():
        pl.semaphore_wait(barrier, len(greet))
        tell(0)

    def loaded(w):
        pltpu.make_async_copy(ins.at[:, w], ins.at[:, w], s_in.at[w]).wait()

    def momentum(w, n, starts, rows):
        for first in starts:
            r = pl.ds(first, rows)
            one = momentum_decay * ins[0, w, r, :].astype(f32) + ins[1, w, r, :].astype(f32)
            one = one.astype(bf16)
            y1_ref[n, r, :] = one
            two = momentum_decay * one.astype(f32) + ins[2, w, r, :].astype(f32)
            y2_ref[n, r, :] = two.astype(bf16)

    for h in range(2):
        for w in range(3):
            @phase("p01")
            def _(h=h, w=w):
                if h == 0:
                    loaded(w)
                momentum(w, turn[w], (h * CHUNK, 128 + h * CHUNK), CHUNK)

            for k in (2 * w, 2 * w + 1):
                row_copies[h][k].start()

    @phase("p01o")
    def _():
        loaded(3)
        momentum(3, lay, (0,), ROWS)

    mates[0].start()

    @phase("w_tell")
    def _():
        pl.semaphore_wait(rounds.at[0], len(told[0]))
        tell(1)

    def heads(ns):
        grams = []
        norms = []
        for n in ns:
            v = y1_ref[n]
            g = lax.dot_general(v, v, (((1,), (1,)), ((), ())), preferred_element_type=f32)
            norm = jnp.sqrt(trace(g)) + norm_epsilon
            grams.append(g * (1.0 / (norm * norm)))
            norms.append(norm)
        for n, q, norm in zip(ns, polynomials(grams, mm), norms):
            high, low = split(q * (math.sqrt(max(ROWS, LATENT)) / norm))
            q1_ref[n, 0] = high
            q1_ref[n, 1] = low

    def gram_of(views, first):
        for i4 in range(4):
            total = None
            for v in views:
                g = lax.dot_general(
                    v[:, pl.ds(i4 * T, T)], v[:, pl.ds(i4 * T, LATENT - i4 * T)],
                    (((0,), (0,)), ((), ())), preferred_element_type=f32)
                total = g if total is None else total + g
            for j4 in range(i4, 4):
                rows = pl.ds(BLOCKS.index((i4, j4)) * T, T)
                value = total[:, (j4 - i4) * T:(j4 - i4 + 1) * T]
                part[rows, :] = value if first else part[rows, :] + value

    mates[0].wait()

    @phase("p_own", True)
    def _():
        gram_of([y2_ref.at[lay], mate], True)

    @phase("w_rows0")
    def _():
        for h in range(2):
            sent = rx.at[h, pl.ds(0, 6 * CHUNK), :]
            send(sent, sent, s_row.at[h], r_row.at[h], partner).wait_send()

    @phase("w_rows", True)
    def _():
        send(rx.at[0], rx.at[0], s_row.at[0], r_row.at[0], partner).wait_recv()

    @phase("p02", True)
    def _():
        gram_of([rx.at[0]], False)

    @phase("w_rows1")
    def _():
        pl.semaphore_wait(rounds.at[1], len(told[1]))
        tell(2)

    @phase("w_rows1b", True)
    def _():
        send(rx.at[1], rx.at[1], s_row.at[1], r_row.at[1], partner).wait_recv()

    @phase("p03", True)
    def _():
        gram_of([rx.at[1]], False)

    rs_copies = []
    for k, (p, t2) in enumerate(team):
        rs_copies.append(send(
            part.at[pl.ds(pl.multiple_of(t2 * PIECE, 8), PIECE), :], rs.at[k],
            s_rs, r_rs, at(*p, 1)))

    pl.semaphore_wait(rounds.at[2], len(told[2]))

    @phase("s_rs", True)
    def _():
        for copy in rs_copies:
            copy.start()
        mates[1].start()

    @phase("p04")
    def _():
        heads((0, 1))

    here = pl.ds(pl.multiple_of(t * PIECE, 8), PIECE)
    ag_copies = [
        send(gath.at[here, :], gath.at[here, :], s_ag, r_ag.at[int(k in FAR)], at(*p, 1))
        for k, (p, _) in enumerate(team)
    ]

    @phase("w_rs", True)
    def _():
        send(rs, rs, s_rs, r_rs, partner).wait()
        total = part[here, :]
        for k in range(15):
            total = total + rs[k]
        gath[here, :] = total

    @phase("s_ag", True)
    def _():
        for copy in ag_copies:
            copy.start()

    @phase("p05")
    def _():
        heads((2, 3))

    def relay(k, t3):
        there = pl.ds(pl.multiple_of(t3 * PIECE, 8), PIECE)
        return send(gath.at[there, :], gath.at[there, :], s_rel, r_rel, partner)

    relays = [(15, t)]
    for k, (di, dj, dz) in enumerate(OFFSETS):
        relays.append((k, (((i + di) % 2) * 2 + (j + dj) % 2) * 4 + (z + 4 - dz) % 4))
    @phase("w_ag", True)
    def _():
        relay(*relays[0]).start()
        for group in range(2):
            ks = [k for k in range(15) if (k in FAR) == (group == 1)]
            some = rs.at[pl.ds(0, len(ks))]
            send(some, some, s_ag, r_ag.at[group], partner).wait_recv()
            for k in ks:
                relay(*relays[k + 1]).start()

    @pl.when(c == 0)
    def _():
        send(gath, gath, s_rel, r_rel, partner).wait_recv()

    @phase("p06")
    def _():
        gram = unpacked(gath[...])
        norm = jnp.sqrt(sum(trace(gram[k:k + T, k:k + T]) for k in range(0, LATENT, T)))
        norm = norm + norm_epsilon
        q = layer_polynomial(
            gram * (1.0 / (norm * norm)), q_full, pl.multiple_of(c * 256, 256))
        q2_ref[0], q2_ref[1] = split((q * (math.sqrt(ALL_ROWS) / norm)).T)

    def columns(core):
        return pl.ds(pl.multiple_of(core * 256, 256), 256)

    def returned(h, k, d, core):
        return send(
            tx.at[h, pl.ds((k * 2 + d) * CHUNK, CHUNK), :],
            got.at[k // 2, pl.ds((k % 2) * 128 + h * CHUNK, CHUNK), columns(core)],
            s_q, r_q, at(*steps[k ^ 1], d))

    @pl.when(c == 0)
    def _():
        mates[1].wait_recv()

    back = []
    for h in range(2):
        @phase("p07")
        def _(h=h):
            w = rx[h]
            tx[h] = (dot(w, q2_ref[0]) + dot(w, q2_ref[1])).astype(bf16)

        for k in range(6):
            for d in range(2):
                back.append(returned(h, k, d, c))
                back[-1].start()

    @phase("p08")
    def _():
        w = mate[...]
        stage[...] = dot(w, q2_ref[0]) + dot(w, q2_ref[1])

    over = [send(stage, own2_ref.at[:, columns(k)], s_own, r_own, partner) for k in (c, 1 - c)]
    over[0].start()

    @phase("p09")
    def _():
        w = y2_ref[lay]
        own2_ref[:, columns(c)] = dot(w, q2_ref[0]) + dot(w, q2_ref[1])
        for n in range(LAYERS):
            v = y1_ref[n]
            o1_ref[n] = dot(q1_ref[n, 0], v) + dot(q1_ref[n, 1], v)

    @phase("w_sent", True)
    def _():
        mates[1].wait_send()
        send(rs, rs, s_ag, r_ag.at[0], partner).wait_send()
        send(gath, gath, s_rel, r_rel, partner).wait_send()

    @phase("w_back")
    def _():
        over[0].wait_send()
        over[1].wait_recv()
        send(got, got, s_q, r_q, partner).wait()


def finish(o1_ref, own2_ref, got, out1, out2, buf, sems):
    x = lax.axis_index("layer")
    head = lax.axis_index("head")
    y, z = head // 8, (head // 2) % 4
    b0, b1 = (x + z) % 2, (y + z) % 2
    copies = [pltpu.make_async_copy(
        own2_ref, out2.at[b0 + 2 * b1], sems.at[LAYERS])]
    for n in range(LAYERS):
        copies.append(pltpu.make_async_copy(o1_ref.at[n], out1.at[n], sems.at[n]))
    for copy in copies:
        copy.start()
    lays = [(1 - b0) + 2 * b1, b0 + 2 * (1 - b1), (1 - b0) + 2 * (1 - b1)]
    for a in range(3):
        buf[a] = got[a].astype(f32)
        copies.append(pltpu.make_async_copy(buf.at[a], out2.at[lays[a]], sems.at[LAYERS + 1 + a]))
        copies[-1].start()
    for copy in copies:
        copy.wait()


def shards(momentum, grad_one, grad_two):
    vmem = pl.BlockSpec(memory_space=pltpu.VMEM)
    hbm = pl.BlockSpec(memory_space=pltpu.MemorySpace.HBM)
    dma = pltpu.SemaphoreType.DMA
    given = pl.pallas_call(
        exchange,
        out_shape=(
            jax.ShapeDtypeStruct((LAYERS, ROWS, LATENT), f32),
            jax.ShapeDtypeStruct((ROWS, LATENT), f32),
            jax.ShapeDtypeStruct((3, ROWS, LATENT), bf16),
        ),
        in_specs=[hbm] * 3,
        out_specs=(vmem,) * 3,
        scratch_shapes=[
            pltpu.VMEM((3, LAYERS, ROWS, LATENT), bf16),
            pltpu.VMEM((LAYERS, ROWS, LATENT), bf16),
            pltpu.VMEM((LAYERS, ROWS, LATENT), bf16),
            pltpu.VMEM((LAYERS, 2, ROWS, ROWS), bf16),
            pltpu.VMEM((2, 12 * CHUNK, LATENT), bf16),
            pltpu.VMEM((ROWS, LATENT), bf16),
            pltpu.VMEM((2, 12 * CHUNK, LATENT // 2), bf16),
            pltpu.VMEM((ROWS, LATENT // 2), f32),
            pltpu.VMEM((2 * HALF, T), f32),
            pltpu.VMEM((15, PIECE, T), f32),
            pltpu.VMEM((2 * HALF, T), f32),
            pltpu.VMEM((LATENT, LATENT), f32),
            pltpu.VMEM((2, LATENT, LATENT // 2), bf16),
            pltpu.SemaphoreType.REGULAR((3,)),
            dma((LAYERS,)), dma((2,)), dma((2,)),
            dma, dma, dma, dma((2,)), dma, dma, dma, dma, dma((2,)), dma((2,)), dma, dma,
        ],
        compiler_params=pltpu.CompilerParams(
            collective_id=0, has_side_effects=True, vmem_limit_bytes=32 << 20),
        name="exchange",
    )(*[
        pltpu.with_memory_space_constraint(v, pltpu.MemorySpace.HBM)
        for v in (momentum, grad_one, grad_two)
    ])
    return pl.pallas_call(
        finish,
        out_shape=(jax.ShapeDtypeStruct((LAYERS, ROWS, LATENT), f32),) * 2,
        in_specs=[vmem] * 3,
        out_specs=(hbm,) * 2,
        scratch_shapes=[pltpu.VMEM((3, ROWS, LATENT), f32), dma((LAYERS + 4,))],
        compiler_params=pltpu.CompilerParams(vmem_limit_bytes=12 << 20),
        name="finish",
    )(*given)


def solution(mesh):
    spec = P(None, ("layer", "head"), None)
    return jax.shard_map(
        shards, mesh=mesh, in_specs=(spec,) * 3, out_specs=(spec,) * 2, check_vma=False
    )
```

```python
import functools
import math

import jax
import jax.numpy as jnp
from jax import lax
from jax.experimental import pallas as pl
from jax.experimental.pallas import tpu as pltpu
from jax.sharding import PartitionSpec as P

NS_ITERS = 5
quintic_a = 3.4445
quintic_b = -4.775
quintic_c = 2.0315
norm_epsilon = 1e-07
momentum_decay = 0.95

bf16 = jnp.bfloat16
f32 = jnp.float32
MESH = pl.DeviceIdType.MESH
LAYERS, ROWS, LATENT = 4, 256, 512
ALL_ROWS = 32768
T = 128
BLOCKS = [(i, j) for i in range(4) for j in range(i, 4)]
HALF = len(BLOCKS) * T // 2
PIECE = HALF // 8
CHUNK = 64
OFFSETS = [(1, 1, 2), (1, 1, 0), (1, 0, 2)]
OFFSETS += [(1, j, z) for z in (1, 3) for j in (0, 1)] + [(1, 0, 0)]
OFFSETS += [(0, 1, 2)] + [(0, j, z) for z in (1, 3) for j in (0, 1)]
OFFSETS += [(0, 1, 0), (0, 0, 2)]
FAR = [0, 1, 2, 8]


def split(x):
    high = x.astype(bf16)
    return high, (x - high.astype(f32)).astype(bf16)


def dot(x, y):
    return jnp.dot(x, y, preferred_element_type=f32)


def dot3(x, y):
    return dot(x[0], y[0]) + (dot(x[0], y[1]) + dot(x[1], y[0]))


def mm(x, y):
    return dot3(x, y)


def mm_even(x, y):
    h = x[0].shape[0] // 2
    top = dot3([t[:h] for t in x], y)
    low = dot3([t[h:] for t in x], [t[:, h:] for t in y])
    return jnp.concatenate([top, jnp.concatenate([top[:, h:].T, low], 1)], 0)


def square_even(x):
    high, low = x
    h = high.shape[0] // 2
    cross = dot(high, low)
    top, last = dot(high[:h], high), dot(high[h:], high[:, h:])
    first = top[:, :h] + (cross[:h, :h] + cross[:h, :h].T)
    side = top[:, h:] + (cross[:h, h:] + cross[h:, :h].T)
    last = last + (cross[h:, h:] + cross[h:, h:].T)
    return jnp.concatenate(
        [jnp.concatenate([first, side], 1), jnp.concatenate([side.T, last], 1)], 0)


def eye(n):
    rows = lax.broadcasted_iota(jnp.int32, (n, n), 0)
    return rows == lax.broadcasted_iota(jnp.int32, (n, n), 1)


def layer_polynomial(gram, scratch, start):
    n = gram.shape[0]
    diag = jnp.where(eye(gram.shape[0]), f32(quintic_a), f32(0.0))
    s, q = gram, None
    for k in range(NS_ITERS):
        part = split(s)
        m = diag + (quintic_b * s + quintic_c * square_even(part))
        if k == 0:
            scratch[...] = m
        ms = split(m)
        if k < NS_ITERS - 1:
            s = mm_even(split(mm_even(part, ms)), ms)
        q = scratch[pl.ds(start, n // 2), :] if k == 0 else dot3(split(q), ms)
    return q


def polynomials(grams, product):
    n = grams[0].shape[0]
    diag = jnp.where(eye(n), f32(quintic_a), f32(0.0))
    s, q = list(grams), [None] * len(grams)
    for k in range(NS_ITERS):
        parts = [split(t) for t in s]
        m = [
            diag + (quintic_b * t + quintic_c * product(u, u)) for t, u in zip(s, parts)
        ]
        ms = [split(t) for t in m]
        if k < NS_ITERS - 1:
            r = [split(product(u, v)) for u, v in zip(parts, ms)]
            s = [product(u, v) for u, v in zip(r, ms)]
        q = m if k == 0 else [product(split(u), v) for u, v in zip(q, ms)]
    return q


def unpacked(blocks):
    tiles = {}
    for b, (i, j) in enumerate(BLOCKS):
        v = blocks[b * T:(b + 1) * T, :]
        tiles[i, j] = v
        if i != j:
            tiles[j, i] = v.T
    return jnp.concatenate(
        [jnp.concatenate([tiles[i, j] for j in range(4)], 1) for i in range(4)], 0)


def trace(x):
    return jnp.sum(jnp.where(eye(x.shape[0]), x, f32(0.0)))


def exchange(
    m_hbm, g1_hbm, g2_hbm, o1_ref, own2_ref, got,
    ins, y1_ref, y2_ref, q1_ref, rx, mate, tx, stage, part, rs, gath,
    q_full, q2_ref, rounds,
    s_in, s_row, r_row, s_rs, r_rs, s_ag, r_ag, s_rel, r_rel,
    s_q, r_q, s_mate, r_mate, s_own, r_own,
):
    x = lax.axis_index("layer")
    head = lax.axis_index("head")
    y, z, c = head // 8, (head // 2) % 4, head % 2
    b0, b1 = (x + z) % 2, (y + z) % 2
    lay = b0 + 2 * b1
    lays = [(1 - b0) + 2 * b1, b0 + 2 * (1 - b1), (1 - b0) + 2 * (1 - b1)]
    i, j = x // 2, y // 2
    t = (i * 2 + j) * 4 + z

    def at(x, y, z, c):
        return (x, (y * 4 + z) * 2 + c)

    steps = []
    for a in range(3):
        for s in range(2):
            d = 1 if s == 0 else 3
            steps.append(((x + d) % 4 if a == 0 else x, (y + d) % 4 if a == 1 else y,
                          (z + d) % 4 if a == 2 else z))
    team = []
    for di, dj, dz in OFFSETS:
        i2, j2, z2 = (i + di) % 2, (j + dj) % 2, (z + dz) % 4
        team.append(((2 * i2 + (b0 + z2) % 2, 2 * j2 + (b1 + z2) % 2, z2),
                     (i2 * 2 + j2) * 4 + z2))
    partner = at(x, y, z, 1 - c)
    always = x < 4

    def phase(name, lead=False):
        def run(body):
            with jax.named_scope(name):
                pl.when(c == 1 if lead else always)(body)
        return run


    turn = lays + [lay]
    loads = [
        [pltpu.make_async_copy(h.at[n], ins.at[k, w], s_in.at[w])
         for k, h in enumerate((m_hbm, g1_hbm, g2_hbm))]
        for w, n in enumerate(turn)
    ]
    for copy in loads[0]:
        copy.start()
    barrier = pltpu.get_barrier_semaphore()
    greet = [partner]
    greet += [at(*p, k) for p in steps for k in (c, 1 - c)]
    for who in greet:
        pl.semaphore_signal(barrier, inc=1, device_id=who, device_id_type=MESH)

    for group in loads[1:]:
        for copy in group:
            copy.start()
    def send(src, dst, ss, rr, who):
        return pltpu.make_async_remote_copy(
            src_ref=src, dst_ref=dst, send_sem=ss, recv_sem=rr, device_id=who,
            device_id_type=MESH)

    row_copies = [
        [send(y2_ref.at[lays[k // 2], pl.ds((k % 2) * 128 + h * CHUNK, CHUNK), :],
              rx.at[h, pl.ds(pl.multiple_of((k * 2 + c) * CHUNK, CHUNK), CHUNK), :],
              s_row.at[h], r_row.at[h], at(*p, 1))
         for k, p in enumerate(steps)]
        for h in range(2)
    ]
    mates = [send(y2_ref.at[lay], mate, s_mate.at[0], r_mate.at[0], partner),
             send(rx, rx, s_mate.at[1], r_mate.at[1], partner)]
    near = [at(*p, c) for p in steps]
    far = [at((x + 2) % 4, y, z, c), at(x, (y + 2) % 4, z, c), at(x, y, (z + 2) % 4, c)]
    told = [near, near + far, far[:1]]

    def tell(k):
        for who in told[k]:
            pl.semaphore_signal(rounds.at[k], inc=1, device_id=who, device_id_type=MESH)

    @phase("w_barrier")
    def _():
        pl.semaphore_wait(barrier, len(greet))
        tell(0)

    def loaded(w):
        pltpu.make_async_copy(ins.at[:, w], ins.at[:, w], s_in.at[w]).wait()

    def momentum(w, n, starts, rows):
        for first in starts:
            r = pl.ds(first, rows)
            one = momentum_decay * ins[0, w, r, :].astype(f32) + ins[1, w, r, :].astype(f32)
            one = one.astype(bf16)
            y1_ref[n, r, :] = one
            two = momentum_decay * one.astype(f32) + ins[2, w, r, :].astype(f32)
            y2_ref[n, r, :] = two.astype(bf16)

    for h in range(2):
        for w in range(3):
            @phase("p01")
            def _(h=h, w=w):
                if h == 0:
                    loaded(w)
                momentum(w, turn[w], (h * CHUNK, 128 + h * CHUNK), CHUNK)

            for k in (2 * w, 2 * w + 1):
                row_copies[h][k].start()

    @phase("p01o")
    def _():
        loaded(3)
        momentum(3, lay, (0,), ROWS)

    mates[0].start()

    @phase("w_tell")
    def _():
        pl.semaphore_wait(rounds.at[0], len(told[0]))
        tell(1)

    def heads(ns):
        grams = []
        norms = []
        for n in ns:
            v = y1_ref[n]
            g = lax.dot_general(v, v, (((1,), (1,)), ((), ())), preferred_element_type=f32)
            norm = jnp.sqrt(trace(g)) + norm_epsilon
            grams.append(g * (1.0 / (norm * norm)))
            norms.append(norm)
        for n, q, norm in zip(ns, polynomials(grams, mm), norms):
            high, low = split(q * (math.sqrt(max(ROWS, LATENT)) / norm))
            q1_ref[n, 0] = high
            q1_ref[n, 1] = low

    def gram_of(views, first):
        for i4 in range(4):
            total = None
            for v in views:
                g = lax.dot_general(
                    v[:, pl.ds(i4 * T, T)], v[:, pl.ds(i4 * T, LATENT - i4 * T)],
                    (((0,), (0,)), ((), ())), preferred_element_type=f32)
                total = g if total is None else total + g
            for j4 in range(i4, 4):
                rows = pl.ds(BLOCKS.index((i4, j4)) * T, T)
                value = total[:, (j4 - i4) * T:(j4 - i4 + 1) * T]
                part[rows, :] = value if first else part[rows, :] + value

    mates[0].wait()

    @phase("p_own", True)
    def _():
        gram_of([y2_ref.at[lay], mate], True)

    @phase("w_rows0")
    def _():
        for h in range(2):
            sent = rx.at[h, pl.ds(0, 6 * CHUNK), :]
            send(sent, sent, s_row.at[h], r_row.at[h], partner).wait_send()

    @phase("w_rows", True)
    def _():
        send(rx.at[0], rx.at[0], s_row.at[0], r_row.at[0], partner).wait_recv()

    @phase("p02", True)
    def _():
        gram_of([rx.at[0]], False)

    @phase("w_rows1")
    def _():
        pl.semaphore_wait(rounds.at[1], len(told[1]))
        tell(2)

    @phase("w_rows1b", True)
    def _():
        send(rx.at[1], rx.at[1], s_row.at[1], r_row.at[1], partner).wait_recv()

    @phase("p03", True)
    def _():
        gram_of([rx.at[1]], False)

    rs_copies = []
    for k, (p, t2) in enumerate(team):
        rs_copies.append(send(
            part.at[pl.ds(pl.multiple_of(t2 * PIECE, 8), PIECE), :], rs.at[k],
            s_rs, r_rs, at(*p, 1)))

    pl.semaphore_wait(rounds.at[2], len(told[2]))

    @phase("s_rs", True)
    def _():
        for copy in rs_copies:
            copy.start()

    @phase("p04")
    def _():
        heads((0, 1))

    here = pl.ds(pl.multiple_of(t * PIECE, 8), PIECE)
    ag_copies = [
        send(gath.at[here, :], gath.at[here, :], s_ag, r_ag.at[int(k in FAR)], at(*p, 1))
        for k, (p, _) in enumerate(team)
    ]

    @phase("w_rs", True)
    def _():
        send(rs, rs, s_rs, r_rs, partner).wait()
        total = part[here, :]
        for k in range(15):
            total = total + rs[k]
        gath[here, :] = total

    @phase("s_ag", True)
    def _():
        for k in FAR + [k for k in range(15) if k not in FAR]:
            ag_copies[k].start()
        mates[1].start()

    @phase("p05")
    def _():
        heads((2, 3))

    def relay(k, t3):
        there = pl.ds(pl.multiple_of(t3 * PIECE, 8), PIECE)
        return send(gath.at[there, :], gath.at[there, :], s_rel, r_rel, partner)

    relays = [(15, t)]
    for k, (di, dj, dz) in enumerate(OFFSETS):
        relays.append((k, (((i + di) % 2) * 2 + (j + dj) % 2) * 4 + (z + 4 - dz) % 4))
    @phase("w_ag", True)
    def _():
        relay(*relays[0]).start()
        for group in range(2):
            ks = [k for k in range(15) if (k in FAR) == (group == 1)]
            some = rs.at[pl.ds(0, len(ks))]
            send(some, some, s_ag, r_ag.at[group], partner).wait_recv()
            for k in ks:
                relay(*relays[k + 1]).start()

    @pl.when(c == 0)
    def _():
        send(gath, gath, s_rel, r_rel, partner).wait_recv()

    @phase("p06")
    def _():
        gram = unpacked(gath[...])
        norm = jnp.sqrt(sum(trace(gram[k:k + T, k:k + T]) for k in range(0, LATENT, T)))
        norm = norm + norm_epsilon
        q = layer_polynomial(
            gram * (1.0 / (norm * norm)), q_full, pl.multiple_of(c * 256, 256))
        q2_ref[0], q2_ref[1] = split((q * (math.sqrt(ALL_ROWS) / norm)).T)

    def columns(core):
        return pl.ds(pl.multiple_of(core * 256, 256), 256)

    def returned(h, k, d, core):
        return send(
            tx.at[h, pl.ds((k * 2 + d) * CHUNK, CHUNK), :],
            got.at[k // 2, pl.ds((k % 2) * 128 + h * CHUNK, CHUNK), columns(core)],
            s_q, r_q, at(*steps[k ^ 1], d))

    @pl.when(c == 0)
    def _():
        mates[1].wait_recv()

    back = []
    for h in range(2):
        @phase("p07")
        def _(h=h):
            w = rx[h]
            tx[h] = (dot(w, q2_ref[0]) + dot(w, q2_ref[1])).astype(bf16)

        for k in range(6):
            for d in range(2):
                back.append(returned(h, k, d, c))
                back[-1].start()

    @phase("p08")
    def _():
        w = mate[...]
        stage[...] = dot(w, q2_ref[0]) + dot(w, q2_ref[1])

    over = [send(stage, own2_ref.at[:, columns(k)], s_own, r_own, partner) for k in (c, 1 - c)]
    over[0].start()

    @phase("p09")
    def _():
        w = y2_ref[lay]
        own2_ref[:, columns(c)] = dot(w, q2_ref[0]) + dot(w, q2_ref[1])
        for n in range(LAYERS):
            v = y1_ref[n]
            o1_ref[n] = dot(q1_ref[n, 0], v) + dot(q1_ref[n, 1], v)

    @phase("w_sent", True)
    def _():
        mates[1].wait_send()
        send(rs, rs, s_ag, r_ag.at[0], partner).wait_send()
        send(gath, gath, s_rel, r_rel, partner).wait_send()

    @phase("w_back")
    def _():
        over[0].wait_send()
        over[1].wait_recv()
        send(got, got, s_q, r_q, partner).wait()


def finish(o1_ref, own2_ref, got, out1, out2, buf, sems):
    x = lax.axis_index("layer")
    head = lax.axis_index("head")
    y, z = head // 8, (head // 2) % 4
    b0, b1 = (x + z) % 2, (y + z) % 2
    copies = [pltpu.make_async_copy(
        own2_ref, out2.at[b0 + 2 * b1], sems.at[LAYERS])]
    for n in range(LAYERS):
        copies.append(pltpu.make_async_copy(o1_ref.at[n], out1.at[n], sems.at[n]))
    for copy in copies:
        copy.start()
    lays = [(1 - b0) + 2 * b1, b0 + 2 * (1 - b1), (1 - b0) + 2 * (1 - b1)]
    for a in range(3):
        buf[a] = got[a].astype(f32)
        copies.append(pltpu.make_async_copy(buf.at[a], out2.at[lays[a]], sems.at[LAYERS + 1 + a]))
        copies[-1].start()
    for copy in copies:
        copy.wait()


def shards(momentum, grad_one, grad_two):
    vmem = pl.BlockSpec(memory_space=pltpu.VMEM)
    hbm = pl.BlockSpec(memory_space=pltpu.MemorySpace.HBM)
    dma = pltpu.SemaphoreType.DMA
    given = pl.pallas_call(
        exchange,
        out_shape=(
            jax.ShapeDtypeStruct((LAYERS, ROWS, LATENT), f32),
            jax.ShapeDtypeStruct((ROWS, LATENT), f32),
            jax.ShapeDtypeStruct((3, ROWS, LATENT), bf16),
        ),
        in_specs=[hbm] * 3,
        out_specs=(vmem,) * 3,
        scratch_shapes=[
            pltpu.VMEM((3, LAYERS, ROWS, LATENT), bf16),
            pltpu.VMEM((LAYERS, ROWS, LATENT), bf16),
            pltpu.VMEM((LAYERS, ROWS, LATENT), bf16),
            pltpu.VMEM((LAYERS, 2, ROWS, ROWS), bf16),
            pltpu.VMEM((2, 12 * CHUNK, LATENT), bf16),
            pltpu.VMEM((ROWS, LATENT), bf16),
            pltpu.VMEM((2, 12 * CHUNK, LATENT // 2), bf16),
            pltpu.VMEM((ROWS, LATENT // 2), f32),
            pltpu.VMEM((2 * HALF, T), f32),
            pltpu.VMEM((15, PIECE, T), f32),
            pltpu.VMEM((2 * HALF, T), f32),
            pltpu.VMEM((LATENT, LATENT), f32),
            pltpu.VMEM((2, LATENT, LATENT // 2), bf16),
            pltpu.SemaphoreType.REGULAR((3,)),
            dma((LAYERS,)), dma((2,)), dma((2,)),
            dma, dma, dma, dma((2,)), dma, dma, dma, dma, dma((2,)), dma((2,)), dma, dma,
        ],
        compiler_params=pltpu.CompilerParams(
            collective_id=0, has_side_effects=True, vmem_limit_bytes=32 << 20),
        name="exchange",
    )(*[
        pltpu.with_memory_space_constraint(v, pltpu.MemorySpace.HBM)
        for v in (momentum, grad_one, grad_two)
    ])
    return pl.pallas_call(
        finish,
        out_shape=(jax.ShapeDtypeStruct((LAYERS, ROWS, LATENT), f32),) * 2,
        in_specs=[vmem] * 3,
        out_specs=(hbm,) * 2,
        scratch_shapes=[pltpu.VMEM((3, ROWS, LATENT), f32), dma((LAYERS + 4,))],
        compiler_params=pltpu.CompilerParams(vmem_limit_bytes=12 << 20),
        name="finish",
    )(*given)


def solution(mesh):
    spec = P(None, ("layer", "head"), None)
    return jax.shard_map(
        shards, mesh=mesh, in_specs=(spec,) * 3, out_specs=(spec,) * 2, check_vma=False
    )
```
